256 devices in a mesh: ctx: 32 (over y, x, core), fsdp: 4 (over z_hi), tp: 2 (over z_lo).
Axes of the slice: x: 4, y: 4, z: 8 (z_hi: 4, z_lo: 2; z = z_hi * 2 + z_lo), core: 2. Of those that a mesh axis runs over, the one named last changes fastest.
Arguments:
- query_gate: bfloat16 [4, 4096, 8192], P('fsdp', 'ctx', 'tp'), may hold values from -6 to 6
- key_proj: bfloat16 [4, 4096, 8192], P('fsdp', 'ctx', 'tp'), may hold values from -6 to 6
- value_proj: bfloat16 [4, 4096, 8192], P('fsdp', 'ctx', 'tp'), may hold values from -6 to 6
- grad_out: bfloat16 [4, 4096, 8192], P('fsdp', 'ctx', 'tp'), may hold values from -6 to 6
- filters: float32 [128, 8192], P('fsdp', 'tp'), may hold values from -0.5 to 0.5
- doc_bounds: int32 [4, 49], P('fsdp'), may hold values from 0 to 4032, as said below
- continues: int32 [4, 32], P('fsdp', 'ctx'), may hold values from 0 to 1, as said below
Outputs:
- grad_query: bfloat16 [4, 4096, 8192], P('fsdp', 'ctx', 'tp')
- grad_key: bfloat16 [4, 4096, 8192], P('fsdp', 'ctx', 'tp')
- grad_value: bfloat16 [4, 4096, 8192], P('fsdp', 'ctx', 'tp')
- grad_filter: float32 [128, 8192], P('fsdp', 'tp')
The draws below stay inside these ranges and needn't reach their ends.
Inputs may be any that keep to these rules, and one draw needn't show every extreme that they name: Each row of doc_bounds increases strictly and begins with 0. continues[w, d] is 0 for d = 0 and wherever a document of window w begins at token d * 128; at other shard edges it may be 0 or 1 (the sequence is cut there or not).
All inputs are finite; a program needn't handle non-finite values.
Results may differ from the reference program's by a relative error of at most 0.0065.
Values may be sent and summed in bfloat16 or wider, within the bound.
A program may use at most 64 MiB of HBM per device.

```python
import math
import jax
import jax.numpy as jnp
from jax import lax

D = 8192
TAPS = 128
TOK_DEV = 128
WIN_TOKENS = 4096
WINDOWS = 4
N_CTX = 32


def doc_layout(key):
    half_shard = TOK_DEV // 2

    def per_window(window):
        window_key = jax.random.fold_in(key, window)
        edge_key = jax.random.fold_in(window_key, 11)
        inner_key = jax.random.fold_in(window_key, 12)
        cut_key = jax.random.fold_in(window_key, 13)
        open_window = window == 0
        edge_order = jax.random.permutation(edge_key, N_CTX - 2) + 1
        edge_shards = edge_order[:N_CTX // 2]
        cut_order = jax.random.permutation(cut_key, N_CTX - 1) + 1
        cut_shards = cut_order[:N_CTX // 4]
        edge_offset = jnp.where(open_window, half_shard, 0).astype(jnp.int32)
        edge_pos = (edge_shards * TOK_DEV).astype(jnp.int32) + edge_offset
        slot_width = half_shard - 1
        slot_count = N_CTX * slot_width
        inner_picks = jax.random.permutation(inner_key, slot_count)[:N_CTX - 1]
        inner_pos = inner_picks // slot_width * TOK_DEV + inner_picks % slot_width + 1
        last_pos = jnp.full((1,), (N_CTX - 1) * TOK_DEV + half_shard, jnp.int32)
        starts = jnp.concatenate([jnp.zeros((1,), jnp.int32), edge_pos, inner_pos.astype(jnp.int32), last_pos])
        starts = jnp.sort(starts)
        shards = jnp.arange(N_CTX, dtype=jnp.int32)
        breaks = jnp.any(edge_shards[None, :] == shards[:, None], axis=1) & jnp.logical_not(open_window)
        cuts = jnp.any(cut_shards[None, :] == shards[:, None], axis=1) & jnp.logical_not(open_window)
        flag_row = jnp.where(breaks | cuts | (shards == 0), 0, 1).astype(jnp.int32)
        return (starts, flag_row)
    return jax.vmap(per_window)(jnp.arange(WINDOWS))


def draw_doc_bounds(key, part):
    return doc_layout(key)[0]


def draw_continues(key, part):
    return doc_layout(key)[1]


def level_of(rng, dims, cuts, low, top_value):
    factor_of, own = 1.0, jax.random.fold_in(rng, 6)
    for axis_at, parts in cuts:
        steps = jnp.exp(jax.random.uniform(jax.random.fold_in(own, axis_at), (parts,), jnp.float32, low / len(cuts), top_value / len(cuts)))
        factor_of = factor_of * jnp.repeat(steps, dims[axis_at] // parts).reshape([-1 if axis == axis_at else 1 for axis in range(len(dims))])
    return factor_of


def bell_draw(stream_key, extent, width, most, pieces=(), kind=jnp.bfloat16):
    values = jax.random.normal(stream_key, extent, jnp.float32) * width
    if len(pieces) > 0:
        values = level_of(stream_key, extent, pieces, -0.22, 0.18) * values
    return jnp.clip(values, min=-most, max=most).astype(kind)


def setup_inputs(seed: int = 0) -> dict:
    key_of = jax.random.split(jax.random.key(seed), 8)
    query_gate = bell_draw(key_of[0], (WINDOWS, WIN_TOKENS, D), 1.0, 6.0, ((0, 4), (1, 32), (2, 2)))
    key_proj = bell_draw(key_of[1], (WINDOWS, WIN_TOKENS, D), 1.0, 6.0, ((0, 4), (1, 32), (2, 2)))
    value_proj = bell_draw(key_of[2], (WINDOWS, WIN_TOKENS, D), 1.0, 6.0, ((0, 4), (1, 32), (2, 2)))
    grad_out = bell_draw(key_of[3], (WINDOWS, WIN_TOKENS, D), 1.0, 6.0, ((0, 4), (1, 32), (2, 2)))
    filters = bell_draw(key_of[4], (TAPS, D), TAPS ** -0.5, 0.5, ((0, 4), (1, 2)), jnp.float32)
    doc_bounds = draw_doc_bounds(jax.random.fold_in(key_of[7], 71), 0)
    continues = draw_continues(jax.random.fold_in(key_of[7], 71), 0)
    return dict(query_gate=query_gate, key_proj=key_proj, value_proj=value_proj, grad_out=grad_out, filters=filters, doc_bounds=doc_bounds, continues=continues)


def effective_starts(bound_row, flag_row):
    positions = jnp.arange(WIN_TOKENS, dtype=jnp.int32)
    below = bound_row[None, :] <= positions[:, None]
    doc_first = lax.optimization_barrier(jnp.max(jnp.where(below, bound_row[None, :], 0), axis=1)).astype(jnp.int32)
    shard_of = positions // TOK_DEV
    own_flag = flag_row[shard_of]
    raised = jnp.maximum(doc_first, (shard_of * TOK_DEV).astype(jnp.int32))
    return jnp.where(own_flag == 1, doc_first, raised).astype(jnp.int32)

def reference(query_gate, key_proj, value_proj, grad_out, filters, doc_bounds, continues):

    def per_window(inputs):
        query_win, key_win, value_win, grad_win, bound_row, flag_row = inputs
        positions = jnp.arange(WIN_TOKENS, dtype=jnp.int32)
        effective = effective_starts(bound_row, flag_row)
        mixed = (key_win.astype(jnp.float32) * value_win.astype(jnp.float32)).astype(jnp.bfloat16)
        mixed_pad = jnp.concatenate([jnp.zeros((TAPS, D), jnp.bfloat16), mixed], axis=0)
        grad_conv = (grad_win.astype(jnp.float32) * query_win.astype(jnp.float32)).astype(jnp.bfloat16)
        grad_pad = jnp.concatenate([grad_conv, jnp.zeros((TAPS, D), jnp.bfloat16)], axis=0)
        start_pad = jnp.concatenate([effective, jnp.full((TAPS,), WIN_TOKENS, jnp.int32)])
        grad_wide = grad_conv.astype(jnp.float32)

        def tap_step(tap_index, state_tuple):
            conv_out, grad_back, filt_grad = state_tuple
            weight_row = lax.dynamic_slice_in_dim(filters, tap_index, 1, 0)
            earlier = lax.dynamic_slice_in_dim(mixed_pad, TAPS - tap_index, WIN_TOKENS, 0).astype(jnp.float32)
            inside = (positions - tap_index >= effective)[:, None]
            conv_out = conv_out + jnp.where(inside, earlier * weight_row, 0.0)
            tap_term = lax.optimization_barrier(jnp.sum(jnp.where(inside, grad_wide * earlier, 0.0), axis=0))
            filt_grad = lax.dynamic_update_slice_in_dim(filt_grad, tap_term[None, :], tap_index, 0)
            ahead_rows = lax.dynamic_slice_in_dim(grad_pad, tap_index, WIN_TOKENS, 0).astype(jnp.float32)
            reaching = (positions >= lax.dynamic_slice_in_dim(start_pad, tap_index, WIN_TOKENS, 0))[:, None]
            grad_back = grad_back + jnp.where(reaching, ahead_rows * weight_row, 0.0)
            return (conv_out, grad_back, filt_grad)
        start_state = (jnp.zeros((WIN_TOKENS, D), jnp.float32), jnp.zeros((WIN_TOKENS, D), jnp.float32), jnp.zeros((TAPS, D), jnp.float32))
        conv_out, grad_back, filt_grad = lax.fori_loop(jnp.int32(0), jnp.int32(TAPS), tap_step, start_state)
        grad_query = (grad_win.astype(jnp.float32) * conv_out).astype(jnp.bfloat16)
        grad_key = (grad_back * value_win.astype(jnp.float32)).astype(jnp.bfloat16)
        grad_value = (grad_back * key_win.astype(jnp.float32)).astype(jnp.bfloat16)
        return (grad_query, grad_key, grad_value, filt_grad)
    grad_query, grad_key, grad_value, filt_all = lax.map(per_window, (query_gate, key_proj, value_proj, grad_out, doc_bounds, continues))
    norm_scale = 1.0 / math.sqrt(WINDOWS * WIN_TOKENS)
    grad_filter = lax.optimization_barrier(jnp.sum(filt_all, axis=0)) * norm_scale
    return (grad_query, grad_key, grad_value, grad_filter)
```

```python
import functools
import math

import jax
import jax.numpy as jnp
import numpy as np
from jax import lax
from jax.experimental import pallas as pl
from jax.experimental.pallas import tpu as pltpu
from jax.sharding import PartitionSpec as P

MESH = pl.DeviceIdType.MESH
T = 128
CW = 512
F32 = jnp.float32
BF16 = jnp.bfloat16
NY, NX, NCORE, NF = 4, 4, 2, 4
BIG = 1e6


def tables():
    theta = np.pi * (np.arange(T) + 0.5)[:, None] / T
    point = np.arange(T)[None, :]

    def pair(offset):
        return np.concatenate([np.cos(theta * (point + offset)), -np.sin(theta * (point + offset))], axis=0)

    forward = pair(0)
    conv_back = pair(T).T / T
    grad_back = pair(-T).T / T
    return [forward.astype(np.float32), conv_back.astype(np.float32), grad_back.astype(np.float32)]


def turn_cos(u):
    u = u - jnp.floor(u + 0.5)
    z = u * u
    total = None
    for n in range(8, -1, -1):
        c = (-1.0) ** n * (2 * math.pi) ** (2 * n) / math.factorial(2 * n)
        total = jnp.full_like(z, c) if total is None else total * z + c
    return total


def turn_sin(u):
    u = u - jnp.floor(u + 0.5)
    z = u * u
    total = None
    for n in range(8, -1, -1):
        c = (-1.0) ** n * (2 * math.pi) ** (2 * n + 1) / math.factorial(2 * n + 1)
        total = jnp.full_like(z, c) if total is None else total * z + c
    return total * u


def dot(a, b):
    return jnp.dot(a, b, preferred_element_type=F32)


def kernel(n_ctx, norm, bounds_ref, cont_ref, fwd_ref, cback_ref, gback_ref, filt_ref, k_hbm, v_hbm, q_hbm, o_hbm,
           gq_hbm, gk_hbm, gv_hbm, gf_ref,
           kb, vb, qb, ob, xb, gb, gm, xp, gn, wb, oq, ok, ov, gfb, r0, p0, r1, p1, r2, p2, r3, fin, r4,
           xg_m, w_m, xp_m, gn_m, conv_m, grad_m, filt_m,
           in_sem, out_sem, hs_sem, hr_sem, ws1, wr1, ws2, wr2, ws3, wr3,
           s0, q0, s1, q1, s2, q2, s3, q3, s4, q4):
    n_chunk = xb.shape[0]
    n_super = n_chunk // 2
    ctx = lax.axis_index("ctx")
    fs = lax.axis_index("fsdp")
    core = lax.rem(ctx, NCORE)
    xi = lax.rem(ctx // NCORE, NX)
    yi = ctx // (NCORE * NX)

    def at(y, x, c):
        return {"ctx": (y * NX + x) * NCORE + c}

    def y_of(d):
        return lax.rem(yi + d, NY)

    def x_of(d):
        return lax.rem(xi + d, NX)

    def f_of(d):
        return lax.rem(fs + d, NF)

    nxt = {"ctx": lax.rem(ctx + 1, n_ctx)}
    prv = {"ctx": lax.rem(ctx + n_ctx - 1, n_ctx)}
    mate = at(yi, xi, 1 - core)
    peers = [nxt, prv, mate]
    peers += [{"fsdp": f_of(d)} for d in (1, 2, 3)]
    peers += [at(y_of(d), xi, c) for d in (1, 2, 3) for c in (core, 1 - core)]
    peers += [at(yi, x_of(d), core) for d in (1, 2, 3)]

    def loads(j):
        cols = pl.ds(pl.multiple_of(j * CW, CW), CW)
        return [pltpu.make_async_copy(src.at[:, cols], dst.at[j], in_sem.at[i, j])
                for i, (src, dst) in enumerate(((k_hbm, kb), (v_hbm, vb), (q_hbm, qb), (o_hbm, ob)))]

    @pl.loop(0, n_chunk)
    def _(j):
        for copy in loads(j):
            copy.start()

    barrier = pltpu.get_barrier_semaphore()
    for peer in peers:
        pl.semaphore_signal(barrier, inc=1, device_id=peer, device_id_type=MESH)

    first = (ctx * T).astype(F32)
    bounds = bounds_ref[...].astype(F32)
    flag = cont_ref[...] == 1
    row = lax.broadcasted_iota(jnp.int32, (T, 1), 0).astype(F32)
    lane = lax.broadcasted_iota(jnp.int32, (1, T), 1).astype(F32)
    low = jnp.max(jnp.where(bounds <= row + first, bounds, 0.0), axis=1, keepdims=True)
    high = jnp.min(jnp.where(bounds > row + first, bounds, BIG), axis=1, keepdims=True)
    begin = jnp.maximum(low - first, 0.0)
    end = jnp.minimum(high - first, float(T))
    size = end - begin
    first_cut = jnp.min(jnp.where(bounds >= first, bounds, BIG), axis=1, keepdims=True) - first
    prev_start = jnp.max(jnp.where(bounds <= first, bounds, 0.0), axis=1, keepdims=True) - first + T
    last_start = jnp.max(jnp.where(bounds <= first + (T - 1), bounds, 0.0), axis=1, keepdims=True) - first
    head_row = jnp.logical_and(row < first_cut, flag)
    tail_row = row >= last_start
    prev_lane = lane >= prev_start
    head_lane = jnp.logical_and(lane < first_cut, flag)

    freq = (row - begin + 0.5) / (2.0 * size)
    same = jnp.logical_and(lane >= begin, lane < end)
    turn = freq * (lane - begin)
    a_re = jnp.where(same, turn_cos(turn), 0.0)
    a_im = jnp.where(same, -turn_sin(turn), 0.0)
    short = lane < size
    turn = freq * lane
    b_re = jnp.where(short, turn_cos(turn), 0.0) / size
    b_im = jnp.where(short, -turn_sin(turn), 0.0) / size
    fwd = fwd_ref[...]
    fwd16 = fwd.astype(BF16)
    xg_m[0:T, :] = a_re.astype(BF16)
    xg_m[T:2 * T, :] = a_im.astype(BF16)
    xg_m[2 * T:4 * T, :] = jnp.where(head_lane, fwd, 0.0).astype(BF16)
    w_m[0:T, :] = b_re.astype(BF16)
    w_m[T:2 * T, :] = b_im.astype(BF16)
    w_m[2 * T:4 * T, :] = fwd16
    xp_m[...] = jnp.where(prev_lane, fwd, 0.0).astype(BF16)
    gn_m[...] = fwd16
    a_back = [a_re.T.astype(BF16), a_im.T.astype(BF16)]
    for m in (conv_m, grad_m):
        m[:, 0:T] = a_back[0]
        m[:, T:2 * T] = a_back[1]
    conv_m[:, 2 * T:4 * T] = jnp.where(head_row, cback_ref[...], 0.0).astype(BF16)
    grad_m[:, 2 * T:4 * T] = jnp.where(tail_row, gback_ref[...], 0.0).astype(BF16)
    filt_m[:, 0:T] = (b_re * norm).T.astype(BF16)
    filt_m[:, T:2 * T] = (b_im * norm).T.astype(BF16)
    filt_m[:, 2 * T:4 * T] = (gback_ref[...] * norm).astype(BF16)

    pl.semaphore_wait(barrier, len(peers))

    own = yi * NCORE + core
    taps = T // NF
    own_rows = pl.ds(pl.multiple_of(fs * taps, taps), taps)
    own_cols = pl.ds(pl.multiple_of(own * CW, CW), CW)
    wb[own, own_rows, :] = filt_ref[:, own_cols].astype(BF16)

    def w_copy(chunk_ref_src, chunk_ref_dst, s, r, dev):
        return pltpu.make_async_remote_copy(src_ref=chunk_ref_src, dst_ref=chunk_ref_dst, send_sem=s, recv_sem=r,
                                            device_id=dev, device_id_type=MESH)

    pending = []
    stage1 = []
    for d in (1, 2, 3):
        copy = w_copy(wb.at[own, own_rows, :], wb.at[own, own_rows, :], ws1.at[d - 1], wr1.at[d - 1], {"fsdp": f_of(d)})
        copy.start()
        stage1.append(copy)

    def halo(j):
        return [w_copy(xb.at[j], xp.at[j], hs_sem.at[0, j], hr_sem.at[0, j], nxt),
                w_copy(gm.at[j], gn.at[j], hs_sem.at[1, j], hr_sem.at[1, j], prv)]

    @pl.loop(0, n_chunk)
    def _(j):
        for copy in loads(j):
            copy.wait()
        xb[j] = (kb[j].astype(F32) * vb[j].astype(F32)).astype(BF16)
        grad_conv = (ob[j].astype(F32) * qb[j].astype(F32)).astype(BF16)
        gb[j] = grad_conv
        gm[j] = jnp.where(head_row, grad_conv.astype(F32), 0.0).astype(BF16)
        for copy in halo(j):
            copy.start()

    for copy in stage1:
        copy.wait()
    stage2 = []
    for d in (1, 2, 3):
        copy = w_copy(wb.at[own], wb.at[own], ws2.at[d - 1], wr2.at[d - 1], at(y_of(d), xi, core))
        copy.start()
        stage2.append(copy)
    stage3 = [w_copy(wb.at[own], wb.at[own], ws3.at[0], wr3.at[0], mate)]
    stage3[0].start()
    for d in (1, 2, 3):
        stage2[d - 1].wait_recv()
        got = lax.rem(yi + NY - d, NY) * NCORE + core
        copy = w_copy(wb.at[got], wb.at[got], ws3.at[d], wr3.at[d], mate)
        copy.start()
        stage3.append(copy)
    for copy in stage3:
        copy.wait_recv()

    def stores(j):
        cols = pl.ds(pl.multiple_of(j * CW, CW), CW)
        return [pltpu.make_async_copy(src.at[j], dst.at[:, cols], out_sem.at[i, j])
                for i, (src, dst) in enumerate(((oq, gq_hbm), (ok, gk_hbm), (ov, gv_hbm)))]

    def times(a, b):
        return [(a[0] * b[0] - a[1] * b[1]).astype(BF16), (a[0] * b[1] + a[1] * b[0]).astype(BF16)]

    def times_conj(a, b):
        return [(a[0] * b[0] + a[1] * b[1]).astype(BF16), (a[1] * b[0] - a[0] * b[1]).astype(BF16)]

    def halves(a):
        return [a[0:T], a[T:2 * T]]

    def chunk(j):
        for copy in halo(j):
            copy.wait_recv()
        for c in range(0, CW, 256):
            cols = pl.ds(c, 256)
            x_in = halves(dot(xg_m[0:2 * T, :], xb[j, :, cols]))
            g_all = dot(xg_m[...], gb[j, :, cols])
            w_all = dot(w_m[...], wb[j, :, cols])
            g_in, g_edge = halves(g_all[0:2 * T]), halves(g_all[2 * T:])
            w_in, w_edge = halves(w_all[0:2 * T]), halves(w_all[2 * T:])
            x_edge = halves(dot(xp_m[...], xp[j, :, cols]))
            g_next = halves(dot(gn_m[...], gn[j, :, cols]))
            filt_f = jnp.concatenate(times_conj(g_in, x_in) + times_conj(g_edge, x_edge), axis=0)
            gfb[j, :, cols] = dot(filt_m[...], filt_f).astype(BF16)
            conv_f = jnp.concatenate(times(x_in, w_in) + times(x_edge, w_edge), axis=0)
            conv = dot(conv_m[...], conv_f)
            oq[j, :, cols] = (ob[j, :, cols].astype(F32) * conv).astype(BF16)
            grad_f = jnp.concatenate(times_conj(g_in, w_in) + times_conj(g_next, w_edge), axis=0)
            grad = dot(grad_m[...], grad_f)
            ok[j, :, cols] = (grad * vb[j, :, cols].astype(F32)).astype(BF16)
            ov[j, :, cols] = (grad * kb[j, :, cols].astype(F32)).astype(BF16)
        for copy in stores(j):
            copy.start()

    copies0, copies1, copies2, copies3, copies4 = {}, {}, {}, {}, {}

    def reduce0(n):
        copies0[n] = w_copy(gfb.at[2 * n + 1 - core], r0.at[n], s0.at[n], q0.at[n], mate)
        copies0[n].start()

    def reduce1(n):
        copies0[n].wait_recv()
        for yq in range(NY):
            cols = pl.ds(yq * T, T)
            p0[n, yq] = (gfb[2 * n + core, :, cols].astype(F32) + r0[n, :, cols].astype(F32)).astype(BF16)
        copies1[n] = []
        for d in (1, 2, 3):
            copy = w_copy(p0.at[n, y_of(d)], r1.at[n, d - 1], s1.at[n, d - 1], q1.at[n, d - 1], at(y_of(d), xi, core))
            copy.start()
            copies1[n].append(copy)

    def reduce2(n):
        for copy in copies1[n]:
            copy.wait_recv()
        total = p0[n, yi].astype(F32)
        for d in range(3):
            total = total + r1[n, d].astype(F32)
        p1[n] = total.astype(BF16)
        copies2[n] = []
        for d in (1, 2, 3):
            rows = pl.ds(pl.multiple_of(f_of(d) * taps, taps), taps)
            copy = w_copy(p1.at[n, rows, :], r2.at[n, d - 1], s2.at[n, d - 1], q2.at[n, d - 1], {"fsdp": f_of(d)})
            copy.start()
            copies2[n].append(copy)

    def reduce3(n):
        for copy in copies2[n]:
            copy.wait_recv()
        total = p1[n, own_rows, :].astype(F32)
        for d in range(3):
            total = total + r2[n, d].astype(F32)
        r3[n, xi] = total.astype(BF16)
        copies3[n] = []
        for d in (1, 2, 3):
            copy = w_copy(r3.at[n, xi], r3.at[n, xi], s3.at[n, d - 1], q3.at[n, d - 1], at(yi, x_of(d), core))
            copy.start()
            copies3[n].append(copy)

    def reduce4(n):
        for copy in copies3[n]:
            copy.wait_recv()
        total = r3[n, 0].astype(F32)
        for x in range(1, NX):
            total = total + r3[n, x].astype(F32)
        r4[n, own] = total
        copies4[n] = []
        others = [(0, 1)] + [(d, c) for d in (1, 2, 3) for c in (0, 1)]
        for i, (d, c) in enumerate(others):
            dev = at(y_of(d), xi, core if c == 0 else 1 - core)
            copy = w_copy(r4.at[n, own], r4.at[n, own], s4.at[n, i], q4.at[n, i], dev)
            copy.start()
            copies4[n].append(copy)

    def reduce5(n):
        for copy in copies4[n]:
            copy.wait_recv()
        for y in range(NY):
            for c in range(NCORE):
                gf_ref[:, pl.ds((2 * n + c) * CW + y * T, T)] = r4[n, y * NCORE + c]

    steps = (reduce1, reduce2, reduce3, reduce4, reduce5)
    for step in range(n_super + len(steps)):
        if step < n_super:
            @pl.loop(2 * step, 2 * step + 2)
            def _(j):
                chunk(j)

            reduce0(step)
        for i, stage in enumerate(steps):
            n = step - 1 - i
            if 0 <= n < n_super:
                stage(n)

    for copy in stage2 + stage3:
        copy.wait_send()
    for n in range(n_super):
        copies0[n].wait_send()
        for copy in copies1[n] + copies2[n] + copies3[n] + copies4[n]:
            copy.wait_send()

    @pl.loop(0, n_chunk)
    def _(j):
        for copy in halo(j):
            copy.wait_send()
        for copy in stores(j):
            copy.wait()


def shards(n_ctx, norm, query_gate, key_proj, value_proj, grad_out, filters, doc_bounds, continues):
    channels = query_gate.shape[2]
    n_chunk = channels // CW
    n_super = n_chunk // 2
    taps = filters.shape[0]
    forward, conv_back, grad_back = (jnp.asarray(t) for t in tables())
    vmem = pl.BlockSpec(memory_space=pltpu.VMEM)
    hbm = pl.BlockSpec(memory_space=pl.ANY)
    big = pltpu.VMEM((n_chunk, T, CW), BF16)
    dma = pltpu.SemaphoreType.DMA
    wide = jax.ShapeDtypeStruct((T, channels), BF16)
    out = pl.pallas_call(
        functools.partial(kernel, n_ctx, norm),
        out_shape=(wide, wide, wide, jax.ShapeDtypeStruct((taps, channels), F32)),
        in_specs=[vmem] * 6 + [hbm] * 4,
        out_specs=(hbm, hbm, hbm, vmem),
        scratch_shapes=[big] * 14 + [
            pltpu.VMEM((n_super, T, CW), BF16),
            pltpu.VMEM((n_super, NY, T, T), BF16),
            pltpu.VMEM((n_super, 3, T, T), BF16),
            pltpu.VMEM((n_super, T, T), BF16),
            pltpu.VMEM((n_super, 3, taps, T), BF16),
            pltpu.VMEM((n_super, taps, T), BF16),
            pltpu.VMEM((n_super, NX, taps, T), BF16),
            pltpu.VMEM((n_super, taps, T), F32),
            pltpu.VMEM((n_super, NY * NCORE, taps, T), F32),
            pltpu.VMEM((4 * T, T), BF16),
            pltpu.VMEM((4 * T, T), BF16),
            pltpu.VMEM((2 * T, T), BF16),
            pltpu.VMEM((2 * T, T), BF16),
            pltpu.VMEM((T, 4 * T), BF16),
            pltpu.VMEM((T, 4 * T), BF16),
            pltpu.VMEM((T, 4 * T), BF16),
            dma((4, n_chunk)), dma((3, n_chunk)), dma((2, n_chunk)), dma((2, n_chunk)),
            dma((3,)), dma((3,)), dma((3,)), dma((3,)), dma((4,)), dma((4,)),
            dma((n_super,)), dma((n_super,)), dma((n_super, 3)), dma((n_super, 3)),
            dma((n_super, 3)), dma((n_super, 3)), dma((n_super, 3)), dma((n_super, 3)),
            dma((n_super, 7)), dma((n_super, 7)),
        ],
        compiler_params=pltpu.CompilerParams(
            collective_id=0, has_side_effects=True, vmem_limit_bytes=48 * 1024 * 1024),
    )(doc_bounds, continues, forward, conv_back, grad_back, filters,
      key_proj[0], value_proj[0], query_gate[0], grad_out[0])
    return out[0][None], out[1][None], out[2][None], out[3]


def solution(mesh):
    n_ctx = mesh.shape["ctx"]
    norm = 1.0 / math.sqrt(mesh.shape["fsdp"] * n_ctx * T)
    wide = P("fsdp", "ctx", "tp")
    return jax.shard_map(
        functools.partial(shards, n_ctx, norm), mesh=mesh,
        in_specs=(wide, wide, wide, wide, P("fsdp", "tp"), P("fsdp", None), P("fsdp", "ctx")),
        out_specs=(wide, wide, wide, P("fsdp", "tp")), check_vma=False)
```

```python
import functools
import math

import jax
import jax.numpy as jnp
from jax import lax
from jax.experimental import pallas as pl
from jax.experimental.pallas import tpu as pltpu
from jax.sharding import PartitionSpec as P

MESH = pl.DeviceIdType.MESH
T = 128
CW = 512
F32 = jnp.float32
BF16 = jnp.bfloat16
NY, NX, NCORE, NF = 4, 4, 2, 4
BIG = 1e6


def turn_cos(u):
    u = u - jnp.floor(u + 0.5)
    z = u * u
    total = None
    for n in range(8, -1, -1):
        c = (-1.0) ** n * (2 * math.pi) ** (2 * n) / math.factorial(2 * n)
        total = jnp.full_like(z, c) if total is None else total * z + c
    return total


def turn_sin(u):
    u = u - jnp.floor(u + 0.5)
    z = u * u
    total = None
    for n in range(8, -1, -1):
        c = (-1.0) ** n * (2 * math.pi) ** (2 * n + 1) / math.factorial(2 * n + 1)
        total = jnp.full_like(z, c) if total is None else total * z + c
    return total * u


def dot(a, b):
    return jnp.dot(a, b, preferred_element_type=F32)


def kernel(n_ctx, norm, bounds_hbm, cont_hbm, filt_hbm, k_hbm, v_hbm, q_hbm, o_hbm,
           gq_out, gk_out, gv_out, gf_out,
           oq, ok, ov, gf_ref, bounds_ref, cont_ref, filt_ref, kb, vb, qb, ob, xb, gb, gm, xp, gn, wb, xi_s, gi_s, filt_f,
           gfb, r0, p0, r1, p1, r2, r3, r4,
           a_m, g0_m, xt_m, xp_m, fwd_m, w_m, conv_m, grad_m, filt_m,
           small_sem, out_sem, in_sem, hs_sem, hr_sem, ws1, wr1, ws2, wr2, ws3, wr3,
           s0, q0, s1, q1, s2, q2, s3, q3, s4, q4):
    n_chunk = xb.shape[0]
    half = n_chunk // 2
    taps = T // NF
    ctx = lax.axis_index("ctx")
    fs = lax.axis_index("fsdp")
    core = lax.rem(ctx, NCORE)
    xi = lax.rem(ctx // NCORE, NX)
    yi = ctx // (NCORE * NX)
    own = yi * NCORE + core
    own_rows = pl.ds(pl.multiple_of(fs * taps, taps), taps)
    own_cols = pl.ds(pl.multiple_of(own * CW, CW), CW)

    def at(y, x, c):
        return {"ctx": (y * NX + x) * NCORE + c}

    def y_of(d):
        return lax.rem(yi + d, NY)

    def x_of(d):
        return lax.rem(xi + d, NX)

    def f_of(d):
        return lax.rem(fs + d, NF)

    def send(src, dst, s, r, dev):
        return pltpu.make_async_remote_copy(src_ref=src, dst_ref=dst, send_sem=s, recv_sem=r,
                                            device_id=dev, device_id_type=MESH)

    nxt = {"ctx": lax.rem(ctx + 1, n_ctx)}
    prv = {"ctx": lax.rem(ctx + n_ctx - 1, n_ctx)}
    mate = at(yi, xi, 1 - core)
    peers = [nxt, prv, mate]
    peers += [{"fsdp": f_of(d)} for d in (1, 2, 3)]
    peers += [at(y_of(d), xi, c) for d in (1, 2, 3) for c in (core, 1 - core)]
    peers += [at(yi, x_of(d), core) for d in (1, 2, 3)]
    barrier = pltpu.get_barrier_semaphore()
    for peer in peers:
        pl.semaphore_signal(barrier, inc=1, device_id=peer, device_id_type=MESH)

    small = [pltpu.make_async_copy(bounds_hbm, bounds_ref, small_sem.at[0]),
             pltpu.make_async_copy(cont_hbm, cont_ref, small_sem.at[1]),
             pltpu.make_async_copy(filt_hbm.at[:, own_cols], filt_ref, small_sem.at[2])]
    for copy in small:
        copy.start()

    def loads(j):
        cols = pl.ds(pl.multiple_of(j * CW, CW), CW)
        return [pltpu.make_async_copy(src.at[:, cols], dst.at[j], in_sem.at[i, j])
                for i, (src, dst) in enumerate(((k_hbm, kb), (v_hbm, vb), (q_hbm, qb), (o_hbm, ob)))]

    @pl.loop(0, n_chunk)
    def _(j):
        for copy in loads(j):
            copy.start()

    for copy in small:
        copy.wait()
    wb[own, own_rows, :] = filt_ref[...].astype(BF16)

    first = (ctx * T).astype(F32)
    bounds = bounds_ref[...].astype(F32)
    flag = cont_ref[...] == 1
    row = lax.broadcasted_iota(jnp.int32, (T, 1), 0).astype(F32)
    lane = lax.broadcasted_iota(jnp.int32, (1, T), 1).astype(F32)
    first_cut = jnp.min(jnp.where(bounds >= first, bounds, BIG), axis=1, keepdims=True) - first
    head_row = jnp.logical_and(row < first_cut, flag)
    head_lane = jnp.logical_and(lane < first_cut, flag)

    @pl.loop(0, n_chunk)
    def _(j):
        for copy in loads(j):
            copy.wait()
        xb[j] = (kb[j].astype(F32) * vb[j].astype(F32)).astype(BF16)
        grad_conv = (ob[j].astype(F32) * qb[j].astype(F32)).astype(BF16)
        gb[j] = grad_conv
        gm[j] = jnp.where(head_row, grad_conv.astype(F32), 0.0).astype(BF16)

    low = jnp.max(jnp.where(bounds <= row + first, bounds, 0.0), axis=1, keepdims=True)
    high = jnp.min(jnp.where(bounds > row + first, bounds, BIG), axis=1, keepdims=True)
    begin = jnp.maximum(low - first, 0.0)
    end = jnp.minimum(high - first, float(T))
    size = end - begin
    prev_start = jnp.max(jnp.where(bounds <= first, bounds, 0.0), axis=1, keepdims=True) - first + T
    last_start = jnp.max(jnp.where(bounds <= first + (T - 1), bounds, 0.0), axis=1, keepdims=True) - first

    freq = (row - begin + 0.5) / (2.0 * size)
    same = jnp.logical_and(lane >= begin, lane < end)
    turn = freq * (lane - begin)
    a_re = jnp.where(same, turn_cos(turn), 0.0)
    a_im = jnp.where(same, -turn_sin(turn), 0.0)
    short = lane < size
    turn = freq * lane
    b_re = jnp.where(short, turn_cos(turn), 0.0) / size
    b_im = jnp.where(short, -turn_sin(turn), 0.0) / size
    turn = (row + 0.5) * lane * (0.5 / T)
    for i, part in enumerate((turn_cos(turn), -turn_sin(turn))):
        rows = pl.ds(i * T, T)
        fwd_m[rows, :] = part.astype(BF16)
        w_m[pl.ds((2 + i) * T, T), :] = part.astype(BF16)
        g0_m[rows, :] = jnp.where(head_lane, part, 0.0).astype(BF16)
        xt_m[rows, :] = jnp.where(lane >= last_start, part, 0.0).astype(BF16)
        xp_m[rows, :] = jnp.where(lane >= prev_start, part, 0.0).astype(BF16)
    for i, (a, b) in enumerate(((a_re, b_re), (a_im, b_im))):
        rows = pl.ds(i * T, T)
        a_m[rows, :] = a.astype(BF16)
        w_m[rows, :] = b.astype(BF16)
        a_back = a.T.astype(BF16)
        conv_m[:, rows] = a_back
        grad_m[:, rows] = a_back
        filt_m[:, rows] = (b * norm).T.astype(BF16)
    turn = (lane + 0.5) * (row + T) * (0.5 / T)
    for i, part in enumerate((turn_cos(turn), -turn_sin(turn))):
        conv_m[:, pl.ds((2 + i) * T, T)] = jnp.where(head_row, part / T, 0.0).astype(BF16)
    turn = (lane + 0.5) * (row - T) * (0.5 / T)
    for i, part in enumerate((turn_cos(turn), -turn_sin(turn))):
        cols = pl.ds((2 + i) * T, T)
        grad_m[:, cols] = jnp.where(row >= last_start, part / T, 0.0).astype(BF16)
        filt_m[:, cols] = (part * (norm / T)).astype(BF16)

    pl.semaphore_wait(barrier, len(peers))

    stage1 = [send(wb.at[own, own_rows, :], wb.at[own, own_rows, :], ws1.at[d - 1], wr1.at[d - 1], {"fsdp": f_of(d)})
              for d in (1, 2, 3)]
    for copy in stage1:
        copy.start()

    def rows_on(j):
        return send(xb.at[j], xp.at[j], hs_sem.at[0, j], hr_sem.at[0, j], nxt)

    def rows_back(j):
        return send(gm.at[j], gn.at[j], hs_sem.at[1, j], hr_sem.at[1, j], prv)

    @pl.loop(0, half)
    def _(i):
        rows_on(i).start()
        rows_back(half + i).start()

    def times(a, b):
        return [(a[0] * b[0] - a[1] * b[1]).astype(BF16), (a[0] * b[1] + a[1] * b[0]).astype(BF16)]

    def times_conj(a, b):
        return [(a[0] * b[0] + a[1] * b[1]).astype(BF16), (a[1] * b[0] - a[0] * b[1]).astype(BF16)]

    def halves(a):
        return [a[0:T], a[T:2 * T]]

    def put(ref, j, start, cols, parts):
        for i, part in enumerate(parts):
            ref[j, pl.ds(start + i * T, T), cols] = part

    blocks = [pl.ds(c, 256) for c in range(0, CW, 256)]

    @pl.loop(0, n_chunk)
    def _(j):
        for cols in blocks:
            x_in = dot(a_m[...], xb[j, :, cols])
            g_in = dot(a_m[...], gb[j, :, cols])
            xi_s[j, :, cols] = x_in
            gi_s[j, :, cols] = g_in
            put(filt_f, j, 0, cols, times_conj(halves(g_in), halves(x_in)))

    for copy in stage1:
        copy.wait()
    stage2 = [send(wb.at[own], wb.at[own], ws2.at[d - 1], wr2.at[d - 1], at(y_of(d), xi, core)) for d in (1, 2, 3)]
    for copy in stage2:
        copy.start()
    stage3 = [send(wb.at[own], wb.at[own], ws3.at[0], wr3.at[0], mate)]
    stage3[0].start()

    def filt_grad(j, wave, side, g_m, g_ref, x_m, x_ref):
        for c, cols in enumerate(blocks):
            g_edge = halves(dot(g_m[...], g_ref[j, :, cols]))
            x_edge = halves(dot(x_m[...], x_ref[j, :, cols]))
            put(filt_f, j, 2 * T, cols, times_conj(g_edge, x_edge))
            gfb[wave, lax.rem(j, NCORE), :, pl.ds(side * CW + c * 256, 256)] = dot(
                filt_m[...], filt_f[j, :, cols]).astype(BF16)

    def wave_work(wave):
        @pl.loop(2 * wave, 2 * wave + 2)
        def _(i):
            rows_on(i).wait_recv()
            rows_on(half + i).start()
            filt_grad(i, wave, 0, g0_m, gb, xp_m, xp)
            rows_back(half + i).wait_recv()
            rows_back(i).start()
            filt_grad(half + i, wave, 1, fwd_m, gn, xt_m, xb)

    sent0, sent1, sent2, sent3, sent4 = {}, {}, {}, {}, {}

    def reduce0(n):
        sent0[n] = [send(gfb.at[n, 1 - core], r0.at[n], s0.at[n], q0.at[n], mate)]
        for copy in sent0[n]:
            copy.start()

    def reduce1(n):
        for copy in sent0[n]:
            copy.wait_recv()
        for yq in range(NY):
            for side in range(2):
                cols = pl.ds(side * CW + yq * T, T)
                p0[n, yq, :, pl.ds(side * T, T)] = (
                    gfb[n, core, :, cols].astype(F32) + r0[n, :, cols].astype(F32)).astype(BF16)
        sent1[n] = [send(p0.at[n, y_of(d)], r1.at[n, d - 1], s1.at[n, d - 1], q1.at[n, d - 1], at(y_of(d), xi, core))
                    for d in (1, 2, 3)]
        for copy in sent1[n]:
            copy.start()

    def reduce2(n):
        for copy in sent1[n]:
            copy.wait_recv()
        total = p0[n, yi].astype(F32)
        for d in range(3):
            total = total + r1[n, d].astype(F32)
        p1[n] = total.astype(BF16)
        sent2[n] = [send(p1.at[n, pl.ds(pl.multiple_of(f_of(d) * taps, taps), taps), :], r2.at[n, d - 1],
                         s2.at[n, d - 1], q2.at[n, d - 1], {"fsdp": f_of(d)}) for d in (1, 2, 3)]
        for copy in sent2[n]:
            copy.start()

    def reduce3(n):
        for copy in sent2[n]:
            copy.wait_recv()
        total = p1[n, own_rows, :].astype(F32)
        for d in range(3):
            total = total + r2[n, d].astype(F32)
        r3[n, xi] = total.astype(BF16)
        sent3[n] = [send(r3.at[n, xi], r3.at[n, xi], s3.at[n, d - 1], q3.at[n, d - 1], at(yi, x_of(d), core))
                    for d in (1, 2, 3)]
        for copy in sent3[n]:
            copy.start()

    def reduce4(n):
        for copy in sent3[n]:
            copy.wait_recv()
        total = r3[n, 0].astype(F32)
        for x in range(1, NX):
            total = total + r3[n, x].astype(F32)
        r4[n, own] = total.astype(BF16)
        others = [(0, 1 - core)] + [(d, c) for d in (1, 2, 3) for c in (core, 1 - core)]
        sent4[n] = [send(r4.at[n, own], r4.at[n, own], s4.at[n, i], q4.at[n, i], at(y_of(d), xi, c))
                    for i, (d, c) in enumerate(others)]
        for copy in sent4[n]:
            copy.start()

    def reduce5(n):
        for copy in sent4[n]:
            copy.wait_recv()
        for y in range(NY):
            for c in range(NCORE):
                for side in range(2):
                    gf_ref[:, pl.ds((side * half + 2 * n + c) * CW + y * T, T)] = (
                        r4[n, y * NCORE + c, :, pl.ds(side * T, T)].astype(F32))

    def conv_and_grad(start, stop):
        @pl.loop(start, stop)
        def _(j):
            for cols in blocks:
                x_in, g_in = halves(xi_s[j, :, cols]), halves(gi_s[j, :, cols])
                w_all = dot(w_m[...], wb[j, :, cols])
                w_in, w_edge = halves(w_all[0:2 * T]), halves(w_all[2 * T:])
                x_edge = halves(dot(xp_m[...], xp[j, :, cols]))
                g_next = halves(dot(fwd_m[...], gn[j, :, cols]))
                conv_f = jnp.concatenate(times(x_in, w_in) + times(x_edge, w_edge), axis=0)
                conv = dot(conv_m[...], conv_f)
                oq[j, :, cols] = (ob[j, :, cols].astype(F32) * conv).astype(BF16)
                grad_f = jnp.concatenate(times_conj(g_in, w_in) + times_conj(g_next, w_edge), axis=0)
                grad = dot(grad_m[...], grad_f)
                ok[j, :, cols] = (grad * vb[j, :, cols].astype(F32)).astype(BF16)
                ov[j, :, cols] = (grad * kb[j, :, cols].astype(F32)).astype(BF16)
            for copy in stores(j):
                copy.start()

    def stores(j):
        cols = pl.ds(pl.multiple_of(j * CW, CW), CW)
        return [pltpu.make_async_copy(src.at[j], dst.at[:, cols], out_sem.at[i, j])
                for i, (src, dst) in enumerate(((oq, gq_out), (ok, gk_out), (ov, gv_out)))]

    wave_work(0)
    reduce0(0)
    wave_work(1)
    reduce0(1)
    reduce1(0)
    reduce1(1)
    for d in (1, 2, 3):
        stage2[d - 1].wait_recv()
        got = lax.rem(yi + NY - d, NY) * NCORE + core
        stage3.append(send(wb.at[got], wb.at[got], ws3.at[d], wr3.at[d], mate))
        stage3[d].start()
    reduce2(0)
    for copy in stage3:
        copy.wait_recv()

    @pl.loop(0, half)
    def _(i):
        rows_on(half + i).wait_recv()
        rows_back(i).wait_recv()

    conv_and_grad(0, 2)
    reduce2(1)
    reduce3(0)
    conv_and_grad(2, 5)
    reduce3(1)
    reduce4(0)
    conv_and_grad(5, n_chunk)
    reduce4(1)
    reduce5(0)
    reduce5(1)
    last = pltpu.make_async_copy(gf_ref, gf_out, small_sem.at[0])
    last.start()

    for copy in stage2 + stage3:
        copy.wait_send()
    for n in range(2):
        for copy in sent0[n] + sent1[n] + sent2[n] + sent3[n] + sent4[n]:
            copy.wait_send()

    @pl.loop(0, n_chunk)
    def _(j):
        rows_on(j).wait_send()
        rows_back(j).wait_send()
        for copy in stores(j):
            copy.wait()

    last.wait()


def write_out(a, b, c, d, a_hbm, b_hbm, c_hbm, d_hbm, va, vb, vc, vd, in_sem, out_sem):
    parts = []
    for i, (src, mid, dst) in enumerate(((a, va, a_hbm), (b, vb, b_hbm), (c, vc, c_hbm), (d, vd, d_hbm))):
        step = src.shape[0] // 2
        for h in range(2):
            rows = pl.ds(h * step, step)
            parts.append((pltpu.make_async_copy(src.at[rows], mid.at[rows], in_sem.at[i, h]),
                          pltpu.make_async_copy(mid.at[rows], dst.at[rows], out_sem.at[i, h])))
    for get, _ in parts:
        get.start()
    for get, put in parts:
        get.wait()
        put.start()
    for _, put in parts:
        put.wait()


def shards(n_ctx, norm, query_gate, key_proj, value_proj, grad_out, filters, doc_bounds, continues):
    channels = query_gate.shape[2]
    n_chunk = channels // CW
    taps = filters.shape[0]
    hbm = pl.BlockSpec(memory_space=pl.ANY)
    pinned = pl.BlockSpec(memory_space=pltpu.HBM)
    dma = pltpu.SemaphoreType.DMA
    wide = jax.ShapeDtypeStruct((T, channels), BF16)
    shapes = (wide, wide, wide, jax.ShapeDtypeStruct((taps, channels), F32))

    def chunks(rows, dtype):
        return pltpu.VMEM((n_chunk, rows, CW), dtype)

    mine = pl.pallas_call(
        functools.partial(kernel, n_ctx, norm),
        out_shape=shapes,
        in_specs=[pinned] * 7,
        out_specs=(hbm,) * 4,
        scratch_shapes=[chunks(T, BF16)] * 3 + [pltpu.VMEM((taps, channels), F32)] + [pltpu.VMEM(doc_bounds.shape, jnp.int32), pltpu.VMEM((1, 1), jnp.int32), pltpu.VMEM((taps, CW), F32)]
        + [chunks(T, BF16)] * 10 + [chunks(2 * T, F32)] * 2 + [chunks(4 * T, BF16)] + [
            pltpu.VMEM((2, NCORE, T, 2 * CW), BF16),
            pltpu.VMEM((2, T, 2 * CW), BF16),
            pltpu.VMEM((2, NY, T, 2 * T), BF16),
            pltpu.VMEM((2, 3, T, 2 * T), BF16),
            pltpu.VMEM((2, T, 2 * T), BF16),
            pltpu.VMEM((2, 3, taps, 2 * T), BF16),
            pltpu.VMEM((2, NX, taps, 2 * T), BF16),
            pltpu.VMEM((2, NY * NCORE, taps, 2 * T), BF16),
        ] + [pltpu.VMEM((2 * T, T), BF16)] * 5 + [pltpu.VMEM((4 * T, T), BF16)] + [pltpu.VMEM((T, 4 * T), BF16)] * 3 + [
            dma((3,)), dma((3, n_chunk)), dma((4, n_chunk)), dma((2, n_chunk)), dma((2, n_chunk)),
            dma((3,)), dma((3,)), dma((3,)), dma((3,)), dma((4,)), dma((4,)),
            dma((2,)), dma((2,)), dma((2, 3)), dma((2, 3)), dma((2, 3)), dma((2, 3)), dma((2, 3)), dma((2, 3)),
            dma((2, 7)), dma((2, 7)),
        ],
        compiler_params=pltpu.CompilerParams(
            collective_id=0, has_side_effects=True, vmem_limit_bytes=62 * 1024 * 1024),
    )(doc_bounds, continues, filters, key_proj[0], value_proj[0], query_gate[0], grad_out[0])
    out = pl.pallas_call(
        write_out, out_shape=shapes, in_specs=[hbm] * 4, out_specs=(pinned,) * 4, scratch_shapes=[pltpu.VMEM(t.shape, t.dtype) for t in shapes] + [dma((4, 2)), dma((4, 2))],
        compiler_params=pltpu.CompilerParams(vmem_limit_bytes=62 * 1024 * 1024),
    )(*mine)
    return out[0][None], out[1][None], out[2][None], out[3]


def solution(mesh):
    n_ctx = mesh.shape["ctx"]
    norm = 1.0 / math.sqrt(mesh.shape["fsdp"] * n_ctx * T)
    wide = P("fsdp", "ctx", "tp")
    return jax.shard_map(
        functools.partial(shards, n_ctx, norm), mesh=mesh,
        in_specs=(wide, wide, wide, wide, P("fsdp", "tp"), P("fsdp", None), P("fsdp", "ctx")),
        out_specs=(wide, wide, wide, P("fsdp", "tp")), check_vma=False)
```

```python
import functools
import math

import jax
import jax.numpy as jnp
from jax import lax
from jax.experimental import pallas as pl
from jax.experimental.pallas import tpu as pltpu
from jax.sharding import PartitionSpec as P

MESH = pl.DeviceIdType.MESH
T = 128
CW = 512
F32 = jnp.float32
BF16 = jnp.bfloat16
NY, NX, NCORE, NF = 4, 4, 2, 4
BIG = 1e6


def turn_cos(u):
    u = u - jnp.floor(u + 0.5)
    z = u * u
    total = None
    for n in range(8, -1, -1):
        c = (-1.0) ** n * (2 * math.pi) ** (2 * n) / math.factorial(2 * n)
        total = jnp.full_like(z, c) if total is None else total * z + c
    return total


def turn_sin(u):
    u = u - jnp.floor(u + 0.5)
    z = u * u
    total = None
    for n in range(8, -1, -1):
        c = (-1.0) ** n * (2 * math.pi) ** (2 * n + 1) / math.factorial(2 * n + 1)
        total = jnp.full_like(z, c) if total is None else total * z + c
    return total * u


def dot(a, b):
    return jnp.dot(a, b, preferred_element_type=F32)


def kernel(n_ctx, norm, bounds_hbm, cont_hbm, filt_hbm, k_hbm, v_hbm, q_hbm, o_hbm,
           oq, ok, ov, gf_ref,
           bounds_ref, cont_ref, filt_ref, kb, vb, qb, ob, gb, edge_out, edge_in, wb, xi_s, gi_s, filt_f,
           gfb, r0, p0, r1, p1, r2, r3, r4,
           a_m, g0_m, xt_m, xp_m, fwd_m, w_m, conv_m, grad_m, filt_m,
           small_sem, in_sem, hs_sem, hr_sem, ws1, wr1, ws2, wr2,
           s0, q0, s1, q1, s2, q2, s3, q3, s4, q4):
    n_chunk = gb.shape[0]
    half = n_chunk // 2
    taps = T // NF
    ctx = lax.axis_index("ctx")
    fs = lax.axis_index("fsdp")
    core = lax.rem(ctx, NCORE)
    xi = lax.rem(ctx // NCORE, NX)
    yi = ctx // (NCORE * NX)
    own = yi * NCORE + core
    own_half = pl.ds(core * half, half)
    own_rows = pl.ds(pl.multiple_of(fs * taps, taps), taps)
    own_cols = pl.ds(pl.multiple_of(core * half * CW, half * CW), half * CW)

    def at(y, x, c):
        return {"ctx": (y * NX + x) * NCORE + c}

    def y_of(d):
        return lax.rem(yi + d, NY)

    def x_of(d):
        return lax.rem(xi + d, NX)

    def f_of(d):
        return lax.rem(fs + d, NF)

    def send(src, dst, s, r, dev):
        return pltpu.make_async_remote_copy(src_ref=src, dst_ref=dst, send_sem=s, recv_sem=r,
                                            device_id=dev, device_id_type=MESH)

    nxt = {"ctx": lax.rem(ctx + 1, n_ctx)}
    prv = {"ctx": lax.rem(ctx + n_ctx - 1, n_ctx)}
    mate = at(yi, xi, 1 - core)
    peers = [nxt, prv, mate]
    peers += [{"fsdp": f_of(d)} for d in (1, 2, 3)]
    peers += [at(y_of(d), xi, c) for d in (1, 2, 3) for c in (core, 1 - core)]
    peers += [at(yi, x_of(d), core) for d in (1, 2, 3)]
    barrier = pltpu.get_barrier_semaphore()
    for peer in peers:
        pl.semaphore_signal(barrier, inc=1, device_id=peer, device_id_type=MESH)

    small = [pltpu.make_async_copy(bounds_hbm, bounds_ref, small_sem.at[0]),
             pltpu.make_async_copy(cont_hbm, cont_ref, small_sem.at[1]),
             pltpu.make_async_copy(filt_hbm.at[:, own_cols], filt_ref, small_sem.at[2])]
    for copy in small:
        copy.start()

    def loads(j):
        cols = pl.ds(pl.multiple_of(j * CW, CW), CW)
        return [pltpu.make_async_copy(src.at[:, cols], dst.at[j], in_sem.at[i, j])
                for i, (src, dst) in enumerate(((k_hbm, kb), (v_hbm, vb), (q_hbm, qb), (o_hbm, ob)))]

    @pl.loop(0, n_chunk)
    def _(j):
        for copy in loads(j):
            copy.start()

    for copy in small:
        copy.wait()
    for i in range(half):
        wb[core * half + i, own_rows, :] = filt_ref[:, i * CW:(i + 1) * CW].astype(BF16)

    first = (ctx * T).astype(F32)
    bounds = bounds_ref[...].astype(F32)
    flag = cont_ref[...] == 1
    row = lax.broadcasted_iota(jnp.int32, (T, 1), 0).astype(F32)
    lane = lax.broadcasted_iota(jnp.int32, (1, T), 1).astype(F32)
    first_cut = jnp.min(jnp.where(bounds >= first, bounds, BIG), axis=1, keepdims=True) - first
    head_row = jnp.logical_and(row < first_cut, flag)
    head_lane = jnp.logical_and(lane < first_cut, flag)

    @pl.loop(0, n_chunk)
    def _(j):
        for copy in loads(j):
            copy.wait()
        edge_out[0, j] = (kb[j].astype(F32) * vb[j].astype(F32)).astype(BF16)
        grad_conv = (ob[j].astype(F32) * qb[j].astype(F32)).astype(BF16)
        gb[j] = grad_conv
        edge_out[1, j] = jnp.where(head_row, grad_conv.astype(F32), 0.0).astype(BF16)

    low = jnp.max(jnp.where(bounds <= row + first, bounds, 0.0), axis=1, keepdims=True)
    high = jnp.min(jnp.where(bounds > row + first, bounds, BIG), axis=1, keepdims=True)
    begin = jnp.maximum(low - first, 0.0)
    end = jnp.minimum(high - first, float(T))
    size = end - begin
    prev_start = jnp.max(jnp.where(bounds <= first, bounds, 0.0), axis=1, keepdims=True) - first + T
    last_start = jnp.max(jnp.where(bounds <= first + (T - 1), bounds, 0.0), axis=1, keepdims=True) - first

    freq = (row - begin + 0.5) / (2.0 * size)
    same = jnp.logical_and(lane >= begin, lane < end)
    turn = freq * (lane - begin)
    a_re = jnp.where(same, turn_cos(turn), 0.0)
    a_im = jnp.where(same, -turn_sin(turn), 0.0)
    short = lane < size
    turn = freq * lane
    b_re = jnp.where(short, turn_cos(turn), 0.0) / size
    b_im = jnp.where(short, -turn_sin(turn), 0.0) / size
    turn = (row + 0.5) * lane * (0.5 / T)
    for i, part in enumerate((turn_cos(turn), -turn_sin(turn))):
        rows = pl.ds(i * T, T)
        fwd_m[rows, :] = part.astype(BF16)
        w_m[pl.ds((2 + i) * T, T), :] = part.astype(BF16)
        g0_m[rows, :] = jnp.where(head_lane, part, 0.0).astype(BF16)
        xt_m[rows, :] = jnp.where(lane >= last_start, part, 0.0).astype(BF16)
        xp_m[rows, :] = jnp.where(lane >= prev_start, part, 0.0).astype(BF16)
    for i, (a, b) in enumerate(((a_re, b_re), (a_im, b_im))):
        rows = pl.ds(i * T, T)
        a_m[rows, :] = a.astype(BF16)
        w_m[rows, :] = b.astype(BF16)
        a_back = a.T.astype(BF16)
        conv_m[:, rows] = a_back
        grad_m[:, rows] = a_back
        filt_m[:, rows] = (b * norm).T.astype(BF16)
    turn = (lane + 0.5) * (row + T) * (0.5 / T)
    for i, part in enumerate((turn_cos(turn), -turn_sin(turn))):
        conv_m[:, pl.ds((2 + i) * T, T)] = jnp.where(head_row, part / T, 0.0).astype(BF16)
    turn = (lane + 0.5) * (row - T) * (0.5 / T)
    for i, part in enumerate((turn_cos(turn), -turn_sin(turn))):
        cols = pl.ds((2 + i) * T, T)
        grad_m[:, cols] = jnp.where(row >= last_start, part / T, 0.0).astype(BF16)
        filt_m[:, cols] = (part * (norm / T)).astype(BF16)

    def times(a, b):
        return [(a[0] * b[0] - a[1] * b[1]).astype(BF16), (a[0] * b[1] + a[1] * b[0]).astype(BF16)]

    def times_conj(a, b):
        return [(a[0] * b[0] + a[1] * b[1]).astype(BF16), (a[1] * b[0] - a[0] * b[1]).astype(BF16)]

    def halves(a):
        return [a[0:T], a[T:2 * T]]

    def put(ref, j, start, cols, parts):
        for i, part in enumerate(parts):
            ref[j, pl.ds(start + i * T, T), cols] = part

    blocks = [pl.ds(c, 256) for c in range(0, CW, 256)]

    @pl.loop(0, n_chunk)
    def _(j):
        for cols in blocks:
            x_in = dot(a_m[...], edge_out[0, j, :, cols])
            g_in = dot(a_m[...], gb[j, :, cols])
            xi_s[j, :, cols] = x_in
            gi_s[j, :, cols] = g_in
            put(filt_f, j, 0, cols, times_conj(halves(g_in), halves(x_in)))

    pl.semaphore_wait(barrier, len(peers))

    wide_rows = wb.at[own_half, own_rows, :]
    stage1 = [send(wide_rows, wide_rows, ws1.at[d - 1], wr1.at[d - 1], {"fsdp": f_of(d)}) for d in (1, 2, 3)]
    stage2 = [send(wide_rows, wide_rows, ws2.at[0], wr2.at[0], mate)]
    for copy in stage1 + stage2:
        copy.start()

    def edge(way, j):
        return send(edge_out.at[way, j], edge_in.at[way, j], hs_sem.at[way, j], hr_sem.at[way, j],
                    {"ctx": lax.rem(ctx + 1 - 2 * way + n_ctx, n_ctx)})

    def early(way, i):
        return edge(way, way * half + i)

    def late(way, i):
        return edge(way, (1 - way) * half + i)

    for part in (early, late):
        for way in (1 - core, core):
            @pl.loop(0, half)
            def _(i):
                part(way, i).start()


    def share_filters():
        for d in (1, 2, 3):
            stage1[d - 1].wait_recv()
            got = wb.at[own_half, pl.ds(pl.multiple_of(lax.rem(fs + NF - d, NF) * taps, taps), taps), :]
            stage2.append(send(got, got, ws2.at[d], wr2.at[d], mate))
            stage2[d].start()

    def filt_grad(wave, side, g_m, g_rows, x_m, x_rows):
        j = side * half + wave
        for c, cols in enumerate(blocks):
            g_edge = halves(dot(g_m[...], g_rows[:, cols]))
            x_edge = halves(dot(x_m[...], x_rows[:, cols]))
            put(filt_f, j, 2 * T, cols, times_conj(g_edge, x_edge))
            gfb[wave, side, :, cols] = dot(filt_m[...], filt_f[j, :, cols]).astype(BF16)

    def wave_work(wave):
        early(0, wave).wait_recv()
        filt_grad(wave, 0, g0_m, gb.at[wave], xp_m, edge_in.at[0, wave])
        early(1, wave).wait_recv()
        filt_grad(wave, 1, fwd_m, edge_in.at[1, half + wave], xt_m, edge_out.at[0, half + wave])

    sent0, sent1, sent2, sent3, sent4 = {}, {}, {}, {}, {}

    def reduce0(n):
        sent0[n] = [send(gfb.at[n, 1 - core], r0.at[n], s0.at[n], q0.at[n], mate)]
        for copy in sent0[n]:
            copy.start()

    def reduce1(n):
        for copy in sent0[n]:
            copy.wait_recv()
        for yq in range(NY):
            cols = pl.ds(yq * T, T)
            p0[n, yq] = (gfb[n, core, :, cols].astype(F32) + r0[n, :, cols].astype(F32)).astype(BF16)
        sent1[n] = [send(p0.at[n, y_of(d)], r1.at[n, d - 1], s1.at[n, d - 1], q1.at[n, d - 1], at(y_of(d), xi, core))
                    for d in (1, 2, 3)]
        for copy in sent1[n]:
            copy.start()

    def reduce2(n):
        for copy in sent1[n]:
            copy.wait_recv()
        total = p0[n, yi].astype(F32)
        for d in range(3):
            total = total + r1[n, d].astype(F32)
        p1[n] = total.astype(BF16)
        sent2[n] = [send(p1.at[n, pl.ds(pl.multiple_of(f_of(d) * taps, taps), taps), :], r2.at[n, d - 1],
                         s2.at[n, d - 1], q2.at[n, d - 1], {"fsdp": f_of(d)}) for d in (1, 2, 3)]
        for copy in sent2[n]:
            copy.start()

    def reduce3(n):
        for copy in sent2[n]:
            copy.wait_recv()
        total = p1[n, own_rows, :].astype(F32)
        for d in range(3):
            total = total + r2[n, d].astype(F32)
        r3[n, xi] = total.astype(BF16)
        sent3[n] = [send(r3.at[n, xi], r3.at[n, xi], s3.at[n, d - 1], q3.at[n, d - 1], at(yi, x_of(d), core))
                    for d in (1, 2, 3)]
        for copy in sent3[n]:
            copy.start()

    def reduce4(n):
        for copy in sent3[n]:
            copy.wait_recv()
        total = r3[n, 0].astype(F32)
        for x in range(1, NX):
            total = total + r3[n, x].astype(F32)
        r4[n, own] = total.astype(BF16)
        others = [(0, 1 - core)] + [(d, c) for d in (1, 2, 3) for c in (core, 1 - core)]
        sent4[n] = [send(r4.at[n, own], r4.at[n, own], s4.at[n, i], q4.at[n, i], at(y_of(d), xi, c))
                    for i, (d, c) in enumerate(others)]
        for copy in sent4[n]:
            copy.start()

    def reduce5(n):
        for copy in sent4[n]:
            copy.wait_recv()
        for y in range(NY):
            for c in range(NCORE):
                gf_ref[:, pl.ds((c * half + n) * CW + y * T, T)] = r4[n, y * NCORE + c].astype(F32)

    def conv_and_grad(start, stop):
        @pl.loop(start, stop)
        def _(j):
            for cols in blocks:
                x_in, g_in = halves(xi_s[j, :, cols]), halves(gi_s[j, :, cols])
                w_all = dot(w_m[...], wb[j, :, cols])
                w_in, w_edge = halves(w_all[0:2 * T]), halves(w_all[2 * T:])
                x_edge = halves(dot(xp_m[...], edge_in[0, j, :, cols]))
                g_next = halves(dot(fwd_m[...], edge_in[1, j, :, cols]))
                conv_f = jnp.concatenate(times(x_in, w_in) + times(x_edge, w_edge), axis=0)
                conv = dot(conv_m[...], conv_f)
                out = pl.ds(pl.multiple_of(j * CW + cols.start, 256), 256)
                oq[:, out] = (ob[j, :, cols].astype(F32) * conv).astype(BF16)
                grad_f = jnp.concatenate(times_conj(g_in, w_in) + times_conj(g_next, w_edge), axis=0)
                grad = dot(grad_m[...], grad_f)
                ok[:, out] = (grad * vb[j, :, cols].astype(F32)).astype(BF16)
                ov[:, out] = (grad * kb[j, :, cols].astype(F32)).astype(BF16)

    wave_work(0)
    reduce0(0)
    wave_work(1)
    reduce0(1)
    reduce1(0)
    wave_work(2)
    reduce0(2)
    reduce1(1)
    wave_work(3)
    reduce0(3)
    reduce1(2)
    reduce1(3)
    reduce2(0)
    reduce2(1)
    reduce2(2)
    reduce2(3)
    share_filters()
    for copy in stage2:
        copy.wait_recv()

    @pl.loop(0, half)
    def _(i):
        late(0, i).wait_recv()
        late(1, i).wait_recv()

    conv_and_grad(0, 2)
    reduce3(0)
    reduce3(1)
    conv_and_grad(2, 4)
    reduce3(2)
    reduce3(3)
    reduce4(0)
    reduce4(1)
    conv_and_grad(4, 6)
    reduce4(2)
    reduce4(3)
    conv_and_grad(6, 8)
    reduce5(0)
    reduce5(1)
    reduce5(2)
    reduce5(3)

    for copy in stage1 + stage2:
        copy.wait_send()
    for n in range(half):
        for copy in sent0[n] + sent1[n] + sent2[n] + sent3[n] + sent4[n]:
            copy.wait_send()

    @pl.loop(0, n_chunk)
    def _(j):
        edge(0, j).wait_send()
        edge(1, j).wait_send()


def write_out(a, b, c, d, a_hbm, b_hbm, c_hbm, d_hbm, sem):
    parts = []
    for i, (src, dst) in enumerate(((a, a_hbm), (b, b_hbm), (c, c_hbm), (d, d_hbm))):
        step = src.shape[0] // 2
        for h in range(2):
            rows = pl.ds(h * step, step)
            parts.append(pltpu.make_async_copy(src.at[rows], dst.at[rows], sem.at[i, h]))
    for put in parts:
        put.start()
    for put in parts:
        put.wait()


def shards(n_ctx, norm, query_gate, key_proj, value_proj, grad_out, filters, doc_bounds, continues):
    channels = query_gate.shape[2]
    n_chunk = channels // CW
    half = n_chunk // 2
    taps = filters.shape[0]
    hbm = pl.BlockSpec(memory_space=pl.ANY)
    pinned = pl.BlockSpec(memory_space=pltpu.HBM)
    dma = pltpu.SemaphoreType.DMA
    wide = jax.ShapeDtypeStruct((T, channels), BF16)
    shapes = (wide, wide, wide, jax.ShapeDtypeStruct((taps, channels), F32))

    def chunks(rows, dtype):
        return pltpu.VMEM((n_chunk, rows, CW), dtype)

    mine = pl.pallas_call(
        functools.partial(kernel, n_ctx, norm),
        out_shape=[pltpu.VMEM(t.shape, t.dtype) for t in shapes],
        in_specs=[pinned] * 7,
        out_specs=[pl.BlockSpec(memory_space=pltpu.VMEM)] * 4,
        scratch_shapes=[pltpu.VMEM(doc_bounds.shape, jnp.int32), pltpu.VMEM((1, 1), jnp.int32), pltpu.VMEM((taps, channels // 2), F32)]
        + [chunks(T, BF16)] * 5 + [pltpu.VMEM((2, n_chunk, T, CW), BF16)] * 2 + [chunks(T, BF16)] + [chunks(2 * T, F32)] * 2 + [chunks(4 * T, BF16)] + [
            pltpu.VMEM((half, NCORE, T, CW), BF16),
            pltpu.VMEM((half, T, CW), BF16),
            pltpu.VMEM((half, NY, T, T), BF16),
            pltpu.VMEM((half, 3, T, T), BF16),
            pltpu.VMEM((half, T, T), BF16),
            pltpu.VMEM((half, 3, taps, T), BF16),
            pltpu.VMEM((half, NX, taps, T), BF16),
            pltpu.VMEM((half, NY * NCORE, taps, T), BF16),
        ] + [pltpu.VMEM((2 * T, T), BF16)] * 5 + [pltpu.VMEM((4 * T, T), BF16)] + [pltpu.VMEM((T, 4 * T), BF16)] * 3 + [
            dma((3,)), dma((4, n_chunk)), dma((2, n_chunk)), dma((2, n_chunk)),
            dma((3,)), dma((3,)), dma((4,)), dma((4,)), dma((half,)), dma((half,)),
        ] + [dma((half, 3))] * 6 + [dma((half, 7))] * 2,
        compiler_params=pltpu.CompilerParams(
            collective_id=0, has_side_effects=True, vmem_limit_bytes=58 * 1024 * 1024),
    )(doc_bounds, continues, filters, key_proj[0], value_proj[0], query_gate[0], grad_out[0])
    out = pl.pallas_call(
        write_out, out_shape=shapes, in_specs=[pl.BlockSpec(memory_space=pltpu.VMEM)] * 4, out_specs=(pinned,) * 4,
        scratch_shapes=[dma((4, 2))], compiler_params=pltpu.CompilerParams(vmem_limit_bytes=48 * 1024 * 1024),
    )(*mine)
    return out[0][None], out[1][None], out[2][None], out[3]


def solution(mesh):
    n_ctx = mesh.shape["ctx"]
    norm = 1.0 / math.sqrt(mesh.shape["fsdp"] * n_ctx * T)
    wide = P("fsdp", "ctx", "tp")
    return jax.shard_map(
        functools.partial(shards, n_ctx, norm), mesh=mesh,
        in_specs=(wide, wide, wide, wide, P("fsdp", "tp"), P("fsdp", None), P("fsdp", "ctx")),
        out_specs=(wide, wide, wide, P("fsdp", "tp")), check_vma=False)
```

```python
import functools
import math

import jax
import jax.numpy as jnp
from jax import lax
from jax.experimental import pallas as pl
from jax.experimental.pallas import tpu as pltpu
from jax.sharding import PartitionSpec as P

MESH = pl.DeviceIdType.MESH
T = 128
CW = 512
F32 = jnp.float32
BF16 = jnp.bfloat16
NY, NX, NCORE, NF = 4, 4, 2, 4
BIG = 1e6


def turn_cos(u):
    u = u - jnp.floor(u + 0.5)
    z = u * u
    total = None
    for n in range(8, -1, -1):
        c = (-1.0) ** n * (2 * math.pi) ** (2 * n) / math.factorial(2 * n)
        total = jnp.full_like(z, c) if total is None else total * z + c
    return total


def turn_sin(u):
    u = u - jnp.floor(u + 0.5)
    z = u * u
    total = None
    for n in range(8, -1, -1):
        c = (-1.0) ** n * (2 * math.pi) ** (2 * n + 1) / math.factorial(2 * n + 1)
        total = jnp.full_like(z, c) if total is None else total * z + c
    return total * u


def dot(a, b):
    return jnp.dot(a, b, preferred_element_type=F32)


def kernel(n_ctx, norm, bounds_hbm, cont_hbm, filt_hbm, k_hbm, v_hbm, q_hbm, o_hbm,
           oq, ok, ov, gf_ref,
           bounds_ref, cont_ref, filt_ref, kb, vb, qb, ob, gb, edge_out, edge_in, wb, xi_s, gi_s, filt_f,
           gfb, r0, p0, r1, p1, r2, r3, r4,
           a_m, g0_m, xt_m, xp_m, fwd_m, w_m, conv_m, grad_m, filt_m,
           small_sem, in_sem, hs_sem, hr_sem, ws1, wr1, ws2, wr2,
           s0, q0, s1, q1, s2, q2, s3, q3, s4, q4):
    n_chunk = gb.shape[0]
    half = n_chunk // 2
    taps = T // NF
    ctx = lax.axis_index("ctx")
    fs = lax.axis_index("fsdp")
    core = lax.rem(ctx, NCORE)
    xi = lax.rem(ctx // NCORE, NX)
    yi = ctx // (NCORE * NX)
    own = yi * NCORE + core
    own_half = pl.ds(core * half, half)
    own_rows = pl.ds(pl.multiple_of(fs * taps, taps), taps)
    own_cols = pl.ds(pl.multiple_of(core * half * CW, half * CW), half * CW)

    def at(y, x, c):
        return {"ctx": (y * NX + x) * NCORE + c}

    def y_of(d):
        return lax.rem(yi + d, NY)

    def x_of(d):
        return lax.rem(xi + d, NX)

    def f_of(d):
        return lax.rem(fs + d, NF)

    def send(src, dst, s, r, dev):
        return pltpu.make_async_remote_copy(src_ref=src, dst_ref=dst, send_sem=s, recv_sem=r,
                                            device_id=dev, device_id_type=MESH)

    nxt = {"ctx": lax.rem(ctx + 1, n_ctx)}
    prv = {"ctx": lax.rem(ctx + n_ctx - 1, n_ctx)}
    mate = at(yi, xi, 1 - core)
    peers = [nxt, prv, mate]
    peers += [{"fsdp": f_of(d)} for d in (1, 2, 3)]
    peers += [at(y_of(d), xi, c) for d in (1, 2, 3) for c in (core, 1 - core)]
    peers += [at(yi, x_of(d), core) for d in (1, 2, 3)]
    barrier = pltpu.get_barrier_semaphore()
    for peer in peers:
        pl.semaphore_signal(barrier, inc=1, device_id=peer, device_id_type=MESH)

    small = [pltpu.make_async_copy(bounds_hbm, bounds_ref, small_sem.at[0]),
             pltpu.make_async_copy(cont_hbm, cont_ref, small_sem.at[1]),
             pltpu.make_async_copy(filt_hbm.at[:, own_cols], filt_ref, small_sem.at[2])]
    for copy in small:
        copy.start()

    def loads(j):
        cols = pl.ds(pl.multiple_of(j * CW, CW), CW)
        return [pltpu.make_async_copy(src.at[:, cols], dst.at[j], in_sem.at[i, j])
                for i, (src, dst) in enumerate(((k_hbm, kb), (v_hbm, vb), (q_hbm, qb), (o_hbm, ob)))]

    @pl.loop(0, n_chunk)
    def _(j):
        for copy in loads(j):
            copy.start()

    for copy in small:
        copy.wait()
    for i in range(half):
        wb[core * half + i, own_rows, :] = filt_ref[:, i * CW:(i + 1) * CW].astype(BF16)

    first = (ctx * T).astype(F32)
    bounds = bounds_ref[...].astype(F32)
    flag = cont_ref[...] == 1
    row = lax.broadcasted_iota(jnp.int32, (T, 1), 0).astype(F32)
    lane = lax.broadcasted_iota(jnp.int32, (1, T), 1).astype(F32)
    first_cut = jnp.min(jnp.where(bounds >= first, bounds, BIG), axis=1, keepdims=True) - first
    head_row = jnp.logical_and(row < first_cut, flag)
    head_lane = jnp.logical_and(lane < first_cut, flag)

    @pl.loop(0, n_chunk)
    def _(j):
        for copy in loads(j):
            copy.wait()
        edge_out[0, j] = (kb[j].astype(F32) * vb[j].astype(F32)).astype(BF16)
        grad_conv = (ob[j].astype(F32) * qb[j].astype(F32)).astype(BF16)
        gb[j] = grad_conv
        edge_out[1, j] = jnp.where(head_row, grad_conv.astype(F32), 0.0).astype(BF16)

    def times(a, b):
        return [(a[0] * b[0] - a[1] * b[1]).astype(BF16), (a[0] * b[1] + a[1] * b[0]).astype(BF16)]

    def times_conj(a, b):
        return [(a[0] * b[0] + a[1] * b[1]).astype(BF16), (a[1] * b[0] - a[0] * b[1]).astype(BF16)]

    def halves(a):
        return [a[0:T], a[T:2 * T]]

    def put(ref, j, start, cols, parts):
        for i, part in enumerate(parts):
            ref[j, pl.ds(start + i * T, T), cols] = part

    pl.semaphore_wait(barrier, len(peers))

    wide_rows = wb.at[own_half, own_rows, :]
    stage1 = [send(wide_rows, wide_rows, ws1.at[d - 1], wr1.at[d - 1], {"fsdp": f_of(d)}) for d in (1, 2, 3)]
    stage2 = [send(wide_rows, wide_rows, ws2.at[0], wr2.at[0], mate)]
    for copy in stage1 + stage2:
        copy.start()

    def edge(way, j):
        return send(edge_out.at[way, j], edge_in.at[way, j], hs_sem.at[way, j], hr_sem.at[way, j],
                    {"ctx": lax.rem(ctx + 1 - 2 * way + n_ctx, n_ctx)})

    def early(way, i):
        return edge(way, way * half + i)

    def late(way, i):
        return edge(way, (1 - way) * half + i)

    def depart_halo(part):
        for way in (1 - core, core):
            @pl.loop(0, half)
            def _(i):
                part(way, i).start()

    depart_halo(early)


    depart_halo(late)

    low = jnp.max(jnp.where(bounds <= row + first, bounds, 0.0), axis=1, keepdims=True)
    high = jnp.min(jnp.where(bounds > row + first, bounds, BIG), axis=1, keepdims=True)
    begin = jnp.maximum(low - first, 0.0)
    end = jnp.minimum(high - first, float(T))
    size = end - begin
    prev_start = jnp.max(jnp.where(bounds <= first, bounds, 0.0), axis=1, keepdims=True) - first + T
    last_start = jnp.max(jnp.where(bounds <= first + (T - 1), bounds, 0.0), axis=1, keepdims=True) - first

    freq = (row - begin + 0.5) / (2.0 * size)
    same = jnp.logical_and(lane >= begin, lane < end)
    turn = freq * (lane - begin)
    a_re = jnp.where(same, turn_cos(turn), 0.0)
    a_im = jnp.where(same, -turn_sin(turn), 0.0)
    short = lane < size
    turn = freq * lane
    b_re = jnp.where(short, turn_cos(turn), 0.0) / size
    b_im = jnp.where(short, -turn_sin(turn), 0.0) / size
    turn = (row + 0.5) * lane * (0.5 / T)
    for i, part in enumerate((turn_cos(turn), -turn_sin(turn))):
        rows = pl.ds(i * T, T)
        fwd_m[rows, :] = part.astype(BF16)
        w_m[pl.ds((2 + i) * T, T), :] = part.astype(BF16)
        g0_m[rows, :] = jnp.where(head_lane, part, 0.0).astype(BF16)
        xt_m[rows, :] = jnp.where(lane >= last_start, part, 0.0).astype(BF16)
        xp_m[rows, :] = jnp.where(lane >= prev_start, part, 0.0).astype(BF16)
    for i, (a, b) in enumerate(((a_re, b_re), (a_im, b_im))):
        rows = pl.ds(i * T, T)
        a_m[rows, :] = a.astype(BF16)
        w_m[rows, :] = b.astype(BF16)
        a_back = a.T.astype(BF16)
        conv_m[:, rows] = a_back
        grad_m[:, rows] = a_back
        filt_m[:, rows] = (b * norm).T.astype(BF16)
    turn = (lane + 0.5) * (row + T) * (0.5 / T)
    for i, part in enumerate((turn_cos(turn), -turn_sin(turn))):
        conv_m[:, pl.ds((2 + i) * T, T)] = jnp.where(head_row, part / T, 0.0).astype(BF16)
    turn = (lane + 0.5) * (row - T) * (0.5 / T)
    for i, part in enumerate((turn_cos(turn), -turn_sin(turn))):
        cols = pl.ds((2 + i) * T, T)
        grad_m[:, cols] = jnp.where(row >= last_start, part / T, 0.0).astype(BF16)
        filt_m[:, cols] = (part * (norm / T)).astype(BF16)

    blocks = [pl.ds(c, 256) for c in range(0, CW, 256)]

    @pl.loop(0, n_chunk)
    def _(j):
        for cols in blocks:
            x_in = dot(a_m[...], edge_out[0, j, :, cols])
            g_in = dot(a_m[...], gb[j, :, cols])
            xi_s[j, :, cols] = x_in
            gi_s[j, :, cols] = g_in
            put(filt_f, j, 0, cols, times_conj(halves(g_in), halves(x_in)))

    def share_filters():
        for d in (1, 2, 3):
            stage1[d - 1].wait_recv()
            got = wb.at[own_half, pl.ds(pl.multiple_of(lax.rem(fs + NF - d, NF) * taps, taps), taps), :]
            stage2.append(send(got, got, ws2.at[d], wr2.at[d], mate))
            stage2[d].start()

    def filt_grad(wave, side, g_m, g_rows, x_m, x_rows):
        j = side * half + wave
        for c, cols in enumerate(blocks):
            g_edge = halves(dot(g_m[...], g_rows[:, cols]))
            x_edge = halves(dot(x_m[...], x_rows[:, cols]))
            put(filt_f, j, 2 * T, cols, times_conj(g_edge, x_edge))
            gfb[wave, side, :, cols] = dot(filt_m[...], filt_f[j, :, cols]).astype(BF16)

    def wave_work(wave):
        early(0, wave).wait_recv()
        filt_grad(wave, 0, g0_m, gb.at[wave], xp_m, edge_in.at[0, wave])
        early(1, wave).wait_recv()
        filt_grad(wave, 1, fwd_m, edge_in.at[1, half + wave], xt_m, edge_out.at[0, half + wave])

    sent0, sent1, sent2, sent3, sent4 = {}, {}, {}, {}, {}

    def reduce0(n):
        sent0[n] = [send(gfb.at[n, 1 - core], r0.at[n], s0.at[n], q0.at[n], mate)]
        for copy in sent0[n]:
            copy.start()

    def reduce1(n):
        for copy in sent0[n]:
            copy.wait_recv()
        for yq in range(NY):
            cols = pl.ds(yq * T, T)
            p0[n, yq] = (gfb[n, core, :, cols].astype(F32) + r0[n, :, cols].astype(F32)).astype(BF16)
        sent1[n] = [send(p0.at[n, y_of(d)], r1.at[n, d - 1], s1.at[n, d - 1], q1.at[n, d - 1], at(y_of(d), xi, core))
                    for d in (1, 2, 3)]
        for copy in sent1[n]:
            copy.start()

    def reduce2(n):
        for copy in sent1[n]:
            copy.wait_recv()
        total = p0[n, yi].astype(F32)
        for d in range(3):
            total = total + r1[n, d].astype(F32)
        p1[n] = total.astype(BF16)
        sent2[n] = [send(p1.at[n, pl.ds(pl.multiple_of(f_of(d) * taps, taps), taps), :], r2.at[n, d - 1],
                         s2.at[n, d - 1], q2.at[n, d - 1], {"fsdp": f_of(d)}) for d in (1, 2, 3)]
        for copy in sent2[n]:
            copy.start()

    def reduce3(n):
        for copy in sent2[n]:
            copy.wait_recv()
        total = p1[n, own_rows, :].astype(F32)
        for d in range(3):
            total = total + r2[n, d].astype(F32)
        r3[n, xi] = total.astype(BF16)
        sent3[n] = [send(r3.at[n, xi], r3.at[n, xi], s3.at[n, d - 1], q3.at[n, d - 1], at(yi, x_of(d), core))
                    for d in (1, 2, 3)]
        for copy in sent3[n]:
            copy.start()

    def reduce4(n):
        for copy in sent3[n]:
            copy.wait_recv()
        total = r3[n, 0].astype(F32)
        for x in range(1, NX):
            total = total + r3[n, x].astype(F32)
        r4[n, own] = total.astype(BF16)
        others = [(0, 1 - core)] + [(d, c) for d in (1, 2, 3) for c in (core, 1 - core)]
        sent4[n] = [send(r4.at[n, own], r4.at[n, own], s4.at[n, i], q4.at[n, i], at(y_of(d), xi, c))
                    for i, (d, c) in enumerate(others)]
        for copy in sent4[n]:
            copy.start()

    def reduce5(n):
        for copy in sent4[n]:
            copy.wait_recv()
        for y in range(NY):
            for c in range(NCORE):
                gf_ref[:, pl.ds((c * half + n) * CW + y * T, T)] = r4[n, y * NCORE + c].astype(F32)

    def conv_and_grad(start, stop):
        @pl.loop(start, stop)
        def _(j):
            for cols in blocks:
                x_in, g_in = halves(xi_s[j, :, cols]), halves(gi_s[j, :, cols])
                w_all = dot(w_m[...], wb[j, :, cols])
                w_in, w_edge = halves(w_all[0:2 * T]), halves(w_all[2 * T:])
                x_edge = halves(dot(xp_m[...], edge_in[0, j, :, cols]))
                g_next = halves(dot(fwd_m[...], edge_in[1, j, :, cols]))
                conv_f = jnp.concatenate(times(x_in, w_in) + times(x_edge, w_edge), axis=0)
                conv = dot(conv_m[...], conv_f)
                out = pl.ds(pl.multiple_of(j * CW + cols.start, 256), 256)
                oq[:, out] = (ob[j, :, cols].astype(F32) * conv).astype(BF16)
                grad_f = jnp.concatenate(times_conj(g_in, w_in) + times_conj(g_next, w_edge), axis=0)
                grad = dot(grad_m[...], grad_f)
                ok[:, out] = (grad * vb[j, :, cols].astype(F32)).astype(BF16)
                ov[:, out] = (grad * kb[j, :, cols].astype(F32)).astype(BF16)

    wave_work(0)
    reduce0(0)
    reduce1(0)
    wave_work(1)
    reduce0(1)
    reduce1(1)
    wave_work(2)
    reduce0(2)
    reduce1(2)
    wave_work(3)
    reduce0(3)
    reduce1(3)
    reduce2(0)
    reduce2(1)
    reduce2(2)
    reduce2(3)
    share_filters()
    for copy in stage2:
        copy.wait_recv()

    @pl.loop(0, half)
    def _(i):
        late(0, i).wait_recv()
        late(1, i).wait_recv()

    conv_and_grad(0, 2)
    reduce3(0)
    reduce3(1)
    conv_and_grad(2, 4)
    reduce3(2)
    reduce3(3)
    reduce4(0)
    reduce4(1)
    conv_and_grad(4, 6)
    reduce4(2)
    reduce4(3)
    conv_and_grad(6, 8)
    reduce5(0)
    reduce5(1)
    reduce5(2)
    reduce5(3)

    for copy in stage1 + stage2:
        copy.wait_send()
    for n in range(half):
        for copy in sent0[n] + sent1[n] + sent2[n] + sent3[n] + sent4[n]:
            copy.wait_send()

    @pl.loop(0, n_chunk)
    def _(j):
        edge(0, j).wait_send()
        edge(1, j).wait_send()


def write_out(a, b, c, d, a_hbm, b_hbm, c_hbm, d_hbm, sem):
    parts = []
    for i, (src, dst) in enumerate(((a, a_hbm), (b, b_hbm), (c, c_hbm), (d, d_hbm))):
        step = src.shape[0] // 2
        for h in range(2):
            rows = pl.ds(h * step, step)
            parts.append(pltpu.make_async_copy(src.at[rows], dst.at[rows], sem.at[i, h]))
    for put in parts:
        put.start()
    for put in parts:
        put.wait()


def shards(n_ctx, norm, query_gate, key_proj, value_proj, grad_out, filters, doc_bounds, continues):
    channels = query_gate.shape[2]
    n_chunk = channels // CW
    half = n_chunk // 2
    taps = filters.shape[0]
    hbm = pl.BlockSpec(memory_space=pl.ANY)
    pinned = pl.BlockSpec(memory_space=pltpu.HBM)
    dma = pltpu.SemaphoreType.DMA
    wide = jax.ShapeDtypeStruct((T, channels), BF16)
    shapes = (wide, wide, wide, jax.ShapeDtypeStruct((taps, channels), F32))

    def chunks(rows, dtype):
        return pltpu.VMEM((n_chunk, rows, CW), dtype)

    mine = pl.pallas_call(
        functools.partial(kernel, n_ctx, norm),
        out_shape=[pltpu.VMEM(t.shape, t.dtype) for t in shapes],
        in_specs=[pinned] * 7,
        out_specs=[pl.BlockSpec(memory_space=pltpu.VMEM)] * 4,
        scratch_shapes=[pltpu.VMEM(doc_bounds.shape, jnp.int32), pltpu.VMEM((1, 1), jnp.int32), pltpu.VMEM((taps, channels // 2), F32)]
        + [chunks(T, BF16)] * 5 + [pltpu.VMEM((2, n_chunk, T, CW), BF16)] * 2 + [chunks(T, BF16)] + [chunks(2 * T, F32)] * 2 + [chunks(4 * T, BF16)] + [
            pltpu.VMEM((half, NCORE, T, CW), BF16),
            pltpu.VMEM((half, T, CW), BF16),
            pltpu.VMEM((half, NY, T, T), BF16),
            pltpu.VMEM((half, 3, T, T), BF16),
            pltpu.VMEM((half, T, T), BF16),
            pltpu.VMEM((half, 3, taps, T), BF16),
            pltpu.VMEM((half, NX, taps, T), BF16),
            pltpu.VMEM((half, NY * NCORE, taps, T), BF16),
        ] + [pltpu.VMEM((2 * T, T), BF16)] * 5 + [pltpu.VMEM((4 * T, T), BF16)] + [pltpu.VMEM((T, 4 * T), BF16)] * 3 + [
            dma((3,)), dma((4, n_chunk)), dma((2, n_chunk)), dma((2, n_chunk)),
            dma((3,)), dma((3,)), dma((4,)), dma((4,)), dma((half,)), dma((half,)),
        ] + [dma((half, 3))] * 6 + [dma((half, 7))] * 2,
        compiler_params=pltpu.CompilerParams(
            collective_id=0, has_side_effects=True, vmem_limit_bytes=58 * 1024 * 1024),
    )(doc_bounds, continues, filters, key_proj[0], value_proj[0], query_gate[0], grad_out[0])
    out = pl.pallas_call(
        write_out, out_shape=shapes, in_specs=[pl.BlockSpec(memory_space=pltpu.VMEM)] * 4, out_specs=(pinned,) * 4,
        scratch_shapes=[dma((4, 2))], compiler_params=pltpu.CompilerParams(vmem_limit_bytes=48 * 1024 * 1024),
    )(*mine)
    return out[0][None], out[1][None], out[2][None], out[3]


def solution(mesh):
    n_ctx = mesh.shape["ctx"]
    norm = 1.0 / math.sqrt(mesh.shape["fsdp"] * n_ctx * T)
    wide = P("fsdp", "ctx", "tp")
    return jax.shard_map(
        functools.partial(shards, n_ctx, norm), mesh=mesh,
        in_specs=(wide, wide, wide, wide, P("fsdp", "tp"), P("fsdp", None), P("fsdp", "ctx")),
        out_specs=(wide, wide, wide, P("fsdp", "tp")), check_vma=False)
```

```python
import functools
import math

import jax
import jax.numpy as jnp
from jax import lax
from jax.experimental import pallas as pl
from jax.experimental.pallas import tpu as pltpu
from jax.sharding import PartitionSpec as P

MESH = pl.DeviceIdType.MESH
T = 128
CW = 512
F32 = jnp.float32
BF16 = jnp.bfloat16
NY, NX, NCORE, NF = 4, 4, 2, 4
BIG = 1e6


def turn_cos(u):
    u = u - jnp.floor(u + 0.5)
    z = u * u
    total = None
    for n in range(8, -1, -1):
        c = (-1.0) ** n * (2 * math.pi) ** (2 * n) / math.factorial(2 * n)
        total = jnp.full_like(z, c) if total is None else total * z + c
    return total


def turn_sin(u):
    u = u - jnp.floor(u + 0.5)
    z = u * u
    total = None
    for n in range(8, -1, -1):
        c = (-1.0) ** n * (2 * math.pi) ** (2 * n + 1) / math.factorial(2 * n + 1)
        total = jnp.full_like(z, c) if total is None else total * z + c
    return total * u


def dot(a, b):
    return jnp.dot(a, b, preferred_element_type=F32)


def kernel(n_ctx, norm, bounds_hbm, cont_hbm, filt_hbm, k_hbm, v_hbm, q_hbm, o_hbm,
           oq, ok, ov, gf_ref,
           bounds_ref, cont_ref, filt_ref, kb, vb, qb, ob, gb, edge_out, edge_in, wb, xi_s, gi_s, filt_f,
           gfb, r0, p0, r1, p1, r2, r3, r4,
           a_m, g0_m, xt_m, xp_m, fwd_m, w_m, conv_m, grad_m, filt_m,
           small_sem, in_sem, hs_sem, hr_sem, ws1, wr1, ws2, wr2,
           s0, q0, s1, q1, s2, q2, s3, q3, s4, q4):
    n_chunk = gb.shape[0]
    half = n_chunk // 2
    taps = T // NF
    ctx = lax.axis_index("ctx")
    fs = lax.axis_index("fsdp")
    core = lax.rem(ctx, NCORE)
    xi = lax.rem(ctx // NCORE, NX)
    yi = ctx // (NCORE * NX)
    own = yi * NCORE + core
    own_half = pl.ds(core * half, half)
    own_rows = pl.ds(pl.multiple_of(fs * taps, taps), taps)
    own_cols = pl.ds(pl.multiple_of(core * half * CW, half * CW), half * CW)

    def at(y, x, c):
        return {"ctx": (y * NX + x) * NCORE + c}

    def y_of(d):
        return lax.rem(yi + d, NY)

    def x_of(d):
        return lax.rem(xi + d, NX)

    def f_of(d):
        return lax.rem(fs + d, NF)

    def send(src, dst, s, r, dev):
        return pltpu.make_async_remote_copy(src_ref=src, dst_ref=dst, send_sem=s, recv_sem=r,
                                            device_id=dev, device_id_type=MESH)

    nxt = {"ctx": lax.rem(ctx + 1, n_ctx)}
    prv = {"ctx": lax.rem(ctx + n_ctx - 1, n_ctx)}
    mate = at(yi, xi, 1 - core)
    peers = [nxt, prv, mate]
    peers += [{"fsdp": f_of(d)} for d in (1, 2, 3)]
    peers += [at(y_of(d), xi, c) for d in (1, 2, 3) for c in (core, 1 - core)]
    peers += [at(yi, x_of(d), core) for d in (1, 2, 3)]
    barrier = pltpu.get_barrier_semaphore()
    for peer in peers:
        pl.semaphore_signal(barrier, inc=1, device_id=peer, device_id_type=MESH)

    small = [pltpu.make_async_copy(bounds_hbm, bounds_ref, small_sem.at[0]),
             pltpu.make_async_copy(cont_hbm, cont_ref, small_sem.at[1]),
             pltpu.make_async_copy(filt_hbm.at[:, own_cols], filt_ref, small_sem.at[2])]
    for copy in small:
        copy.start()

    def loads(j):
        cols = pl.ds(pl.multiple_of(j * CW, CW), CW)
        return [pltpu.make_async_copy(src.at[:, cols], dst.at[j], in_sem.at[i, j])
                for i, (src, dst) in enumerate(((k_hbm, kb), (v_hbm, vb), (q_hbm, qb), (o_hbm, ob)))]

    @pl.loop(0, n_chunk)
    def _(j):
        for copy in loads(j):
            copy.start()

    for copy in small:
        copy.wait()
    for i in range(half):
        wb[core * half + i, own_rows, :] = filt_ref[:, i * CW:(i + 1) * CW].astype(BF16)

    first = (ctx * T).astype(F32)
    bounds = bounds_ref[...].astype(F32)
    flag = cont_ref[...] == 1
    row = lax.broadcasted_iota(jnp.int32, (T, 1), 0).astype(F32)
    lane = lax.broadcasted_iota(jnp.int32, (1, T), 1).astype(F32)
    first_cut = jnp.min(jnp.where(bounds >= first, bounds, BIG), axis=1, keepdims=True) - first
    head_row = jnp.logical_and(row < first_cut, flag)
    head_lane = jnp.logical_and(lane < first_cut, flag)

    @pl.loop(0, n_chunk)
    def _(j):
        for copy in loads(j):
            copy.wait()
        edge_out[0, j] = (kb[j].astype(F32) * vb[j].astype(F32)).astype(BF16)
        grad_conv = (ob[j].astype(F32) * qb[j].astype(F32)).astype(BF16)
        gb[j] = grad_conv
        edge_out[1, j] = jnp.where(head_row, grad_conv.astype(F32), 0.0).astype(BF16)

    def times(a, b):
        return [(a[0] * b[0] - a[1] * b[1]).astype(BF16), (a[0] * b[1] + a[1] * b[0]).astype(BF16)]

    def times_conj(a, b):
        return [(a[0] * b[0] + a[1] * b[1]).astype(BF16), (a[1] * b[0] - a[0] * b[1]).astype(BF16)]

    def halves(a):
        return [a[0:T], a[T:2 * T]]

    def put(ref, j, start, cols, parts):
        for i, part in enumerate(parts):
            ref[j, pl.ds(start + i * T, T), cols] = part

    pl.semaphore_wait(barrier, len(peers))

    wide_rows = wb.at[own_half, own_rows, :]
    stage1 = [send(wide_rows, wide_rows, ws1.at[d - 1], wr1.at[d - 1], {"fsdp": f_of(d)}) for d in (1, 2, 3)]
    stage2 = [send(wide_rows, wide_rows, ws2.at[0], wr2.at[0], mate)]
    for copy in stage1 + stage2:
        copy.start()

    def edge(way, j):
        return send(edge_out.at[way, j], edge_in.at[way, j], hs_sem.at[way, j], hr_sem.at[way, j],
                    {"ctx": lax.rem(ctx + 1 - 2 * way + n_ctx, n_ctx)})

    def early(way, i):
        return edge(way, way * half + i)

    def late(way, i):
        return edge(way, (1 - way) * half + i)

    def depart_halo(part):
        for way in (1 - core, core):
            @pl.loop(0, half)
            def _(i):
                part(way, i).start()

    depart_halo(early)


    depart_halo(late)

    low = jnp.max(jnp.where(bounds <= row + first, bounds, 0.0), axis=1, keepdims=True)
    high = jnp.min(jnp.where(bounds > row + first, bounds, BIG), axis=1, keepdims=True)
    begin = jnp.maximum(low - first, 0.0)
    end = jnp.minimum(high - first, float(T))
    size = end - begin
    prev_start = jnp.max(jnp.where(bounds <= first, bounds, 0.0), axis=1, keepdims=True) - first + T
    last_start = jnp.max(jnp.where(bounds <= first + (T - 1), bounds, 0.0), axis=1, keepdims=True) - first

    freq = (row - begin + 0.5) / (2.0 * size)
    same = jnp.logical_and(lane >= begin, lane < end)
    turn = freq * (lane - begin)
    a_re = jnp.where(same, turn_cos(turn), 0.0)
    a_im = jnp.where(same, -turn_sin(turn), 0.0)
    short = lane < size
    turn = freq * lane
    b_re = jnp.where(short, turn_cos(turn), 0.0) / size
    b_im = jnp.where(short, -turn_sin(turn), 0.0) / size
    turn = (row + 0.5) * lane * (0.5 / T)
    for i, part in enumerate((turn_cos(turn), -turn_sin(turn))):
        rows = pl.ds(i * T, T)
        fwd_m[rows, :] = part.astype(BF16)
        w_m[pl.ds((2 + i) * T, T), :] = part.astype(BF16)
        g0_m[rows, :] = jnp.where(head_lane, part, 0.0).astype(BF16)
        xt_m[rows, :] = jnp.where(lane >= last_start, part, 0.0).astype(BF16)
        xp_m[rows, :] = jnp.where(lane >= prev_start, part, 0.0).astype(BF16)
    for i, (a, b) in enumerate(((a_re, b_re), (a_im, b_im))):
        rows = pl.ds(i * T, T)
        a_m[rows, :] = a.astype(BF16)
        w_m[rows, :] = b.astype(BF16)
        a_back = a.T.astype(BF16)
        conv_m[:, rows] = a_back
        grad_m[:, rows] = a_back
        filt_m[:, rows] = (b * norm).T.astype(BF16)
    turn = (lane + 0.5) * (row + T) * (0.5 / T)
    for i, part in enumerate((turn_cos(turn), -turn_sin(turn))):
        conv_m[:, pl.ds((2 + i) * T, T)] = jnp.where(head_row, part / T, 0.0).astype(BF16)
    turn = (lane + 0.5) * (row - T) * (0.5 / T)
    for i, part in enumerate((turn_cos(turn), -turn_sin(turn))):
        cols = pl.ds((2 + i) * T, T)
        grad_m[:, cols] = jnp.where(row >= last_start, part / T, 0.0).astype(BF16)
        filt_m[:, cols] = (part * (norm / T)).astype(BF16)

    blocks = [pl.ds(c, 256) for c in range(0, CW, 256)]

    @pl.loop(0, n_chunk)
    def _(j):
        for cols in blocks:
            x_in = dot(a_m[...], edge_out[0, j, :, cols])
            g_in = dot(a_m[...], gb[j, :, cols])
            xi_s[j, :, cols] = x_in
            gi_s[j, :, cols] = g_in
            put(filt_f, j, 0, cols, times_conj(halves(g_in), halves(x_in)))

    def share_filters():
        for d in (1, 2, 3):
            stage1[d - 1].wait_recv()
            got = wb.at[own_half, pl.ds(pl.multiple_of(lax.rem(fs + NF - d, NF) * taps, taps), taps), :]
            stage2.append(send(got, got, ws2.at[d], wr2.at[d], mate))
            stage2[d].start()

    def filt_grad(wave, side, g_m, g_rows, x_m, x_rows):
        j = side * half + wave
        for c, cols in enumerate(blocks):
            g_edge = halves(dot(g_m[...], g_rows[:, cols]))
            x_edge = halves(dot(x_m[...], x_rows[:, cols]))
            put(filt_f, j, 2 * T, cols, times_conj(g_edge, x_edge))
            gfb[wave, side, :, cols] = dot(filt_m[...], filt_f[j, :, cols]).astype(BF16)

    def wave_work(wave):
        early(0, wave).wait_recv()
        filt_grad(wave, 0, g0_m, gb.at[wave], xp_m, edge_in.at[0, wave])
        early(1, wave).wait_recv()
        filt_grad(wave, 1, fwd_m, edge_in.at[1, half + wave], xt_m, edge_out.at[0, half + wave])

    sent0, sent1, sent2, sent3, sent4 = {}, {}, {}, {}, {}

    def reduce0(n):
        sent0[n] = [send(gfb.at[n, 1 - core], r0.at[n], s0.at[n], q0.at[n], mate)]
        for copy in sent0[n]:
            copy.start()

    def reduce1(n):
        for copy in sent0[n]:
            copy.wait_recv()
        for yq in range(NY):
            cols = pl.ds(yq * T, T)
            p0[n, yq] = (gfb[n, core, :, cols].astype(F32) + r0[n, :, cols].astype(F32)).astype(BF16)
        sent1[n] = [send(p0.at[n, y_of(d)], r1.at[n, d - 1], s1.at[n, d - 1], q1.at[n, d - 1], at(y_of(d), xi, core))
                    for d in (1, 2, 3)]
        for copy in sent1[n]:
            copy.start()

    def reduce2(n):
        for copy in sent1[n]:
            copy.wait_recv()
        total = p0[n, yi].astype(F32)
        for d in range(3):
            total = total + r1[n, d].astype(F32)
        p1[n] = total.astype(BF16)
        sent2[n] = [send(p1.at[n, pl.ds(pl.multiple_of(f_of(d) * taps, taps), taps), :], r2.at[n, d - 1],
                         s2.at[n, d - 1], q2.at[n, d - 1], {"fsdp": f_of(d)}) for d in (1, 2, 3)]
        for copy in sent2[n]:
            copy.start()

    def reduce3(n):
        for copy in sent2[n]:
            copy.wait_recv()
        total = p1[n, own_rows, :].astype(F32)
        for d in range(3):
            total = total + r2[n, d].astype(F32)
        r3[n, xi] = total.astype(BF16)
        sent3[n] = [send(r3.at[n, xi], r3.at[n, xi], s3.at[n, d - 1], q3.at[n, d - 1], at(yi, x_of(d), core))
                    for d in (1, 2, 3)]
        for copy in sent3[n]:
            copy.start()

    def reduce4(n):
        for copy in sent3[n]:
            copy.wait_recv()
        total = r3[n, 0].astype(F32)
        for x in range(1, NX):
            total = total + r3[n, x].astype(F32)
        r4[n, own] = total.astype(BF16)
        others = [(0, 1 - core)] + [(d, c) for d in (1, 2, 3) for c in (core, 1 - core)]
        sent4[n] = [send(r4.at[n, own], r4.at[n, own], s4.at[n, i], q4.at[n, i], at(y_of(d), xi, c))
                    for i, (d, c) in enumerate(others)]
        for copy in sent4[n]:
            copy.start()

    def reduce5(n):
        for copy in sent4[n]:
            copy.wait_recv()
        for y in range(NY):
            for c in range(NCORE):
                gf_ref[:, pl.ds((c * half + n) * CW + y * T, T)] = r4[n, y * NCORE + c].astype(F32)

    def conv_and_grad(start, stop):
        @pl.loop(start, stop)
        def _(j):
            for cols in blocks:
                x_in, g_in = halves(xi_s[j, :, cols]), halves(gi_s[j, :, cols])
                w_all = dot(w_m[...], wb[j, :, cols])
                w_in, w_edge = halves(w_all[0:2 * T]), halves(w_all[2 * T:])
                x_edge = halves(dot(xp_m[...], edge_in[0, j, :, cols]))
                g_next = halves(dot(fwd_m[...], edge_in[1, j, :, cols]))
                conv_f = jnp.concatenate(times(x_in, w_in) + times(x_edge, w_edge), axis=0)
                conv = dot(conv_m[...], conv_f)
                out = pl.ds(pl.multiple_of(j * CW + cols.start, 256), 256)
                oq[:, out] = (ob[j, :, cols].astype(F32) * conv).astype(BF16)
                grad_f = jnp.concatenate(times_conj(g_in, w_in) + times_conj(g_next, w_edge), axis=0)
                grad = dot(grad_m[...], grad_f)
                ok[:, out] = (grad * vb[j, :, cols].astype(F32)).astype(BF16)
                ov[:, out] = (grad * kb[j, :, cols].astype(F32)).astype(BF16)

    wave_work(0)
    reduce0(0)
    reduce1(0)
    wave_work(1)
    reduce0(1)
    reduce1(1)
    wave_work(2)
    reduce0(2)
    reduce1(2)
    wave_work(3)
    reduce0(3)
    reduce1(3)
    reduce2(0)
    reduce2(1)
    reduce2(2)
    reduce2(3)
    share_filters()
    for copy in stage2:
        copy.wait_recv()

    @pl.loop(0, half)
    def _(i):
        late(0, i).wait_recv()
        late(1, i).wait_recv()

    conv_and_grad(0, 1)
    reduce3(0)
    reduce3(1)
    conv_and_grad(1, 2)
    reduce3(2)
    reduce3(3)
    conv_and_grad(2, 4)
    reduce4(0)
    reduce4(1)
    conv_and_grad(4, 5)
    reduce4(2)
    reduce4(3)
    conv_and_grad(5, n_chunk)
    reduce5(0)
    reduce5(1)
    reduce5(2)
    reduce5(3)

    for copy in stage1 + stage2:
        copy.wait_send()
    for n in range(half):
        for copy in sent0[n] + sent1[n] + sent2[n] + sent3[n] + sent4[n]:
            copy.wait_send()

    @pl.loop(0, n_chunk)
    def _(j):
        edge(0, j).wait_send()
        edge(1, j).wait_send()


def write_out(a, b, c, d, a_hbm, b_hbm, c_hbm, d_hbm, sem):
    parts = []
    for i, (src, dst) in enumerate(((a, a_hbm), (b, b_hbm), (c, c_hbm), (d, d_hbm))):
        step = src.shape[0] // 2
        for h in range(2):
            rows = pl.ds(h * step, step)
            parts.append(pltpu.make_async_copy(src.at[rows], dst.at[rows], sem.at[i, h]))
    for put in parts:
        put.start()
    for put in parts:
        put.wait()


def shards(n_ctx, norm, query_gate, key_proj, value_proj, grad_out, filters, doc_bounds, continues):
    channels = query_gate.shape[2]
    n_chunk = channels // CW
    half = n_chunk // 2
    taps = filters.shape[0]
    hbm = pl.BlockSpec(memory_space=pl.ANY)
    pinned = pl.BlockSpec(memory_space=pltpu.HBM)
    dma = pltpu.SemaphoreType.DMA
    wide = jax.ShapeDtypeStruct((T, channels), BF16)
    shapes = (wide, wide, wide, jax.ShapeDtypeStruct((taps, channels), F32))

    def chunks(rows, dtype):
        return pltpu.VMEM((n_chunk, rows, CW), dtype)

    mine = pl.pallas_call(
        functools.partial(kernel, n_ctx, norm),
        out_shape=[pltpu.VMEM(t.shape, t.dtype) for t in shapes],
        in_specs=[pinned] * 7,
        out_specs=[pl.BlockSpec(memory_space=pltpu.VMEM)] * 4,
        scratch_shapes=[pltpu.VMEM(doc_bounds.shape, jnp.int32), pltpu.VMEM((1, 1), jnp.int32), pltpu.VMEM((taps, channels // 2), F32)]
        + [chunks(T, BF16)] * 5 + [pltpu.VMEM((2, n_chunk, T, CW), BF16)] * 2 + [chunks(T, BF16)] + [chunks(2 * T, F32)] * 2 + [chunks(4 * T, BF16)] + [
            pltpu.VMEM((half, NCORE, T, CW), BF16),
            pltpu.VMEM((half, T, CW), BF16),
            pltpu.VMEM((half, NY, T, T), BF16),
            pltpu.VMEM((half, 3, T, T), BF16),
            pltpu.VMEM((half, T, T), BF16),
            pltpu.VMEM((half, 3, taps, T), BF16),
            pltpu.VMEM((half, NX, taps, T), BF16),
            pltpu.VMEM((half, NY * NCORE, taps, T), BF16),
        ] + [pltpu.VMEM((2 * T, T), BF16)] * 5 + [pltpu.VMEM((4 * T, T), BF16)] + [pltpu.VMEM((T, 4 * T), BF16)] * 3 + [
            dma((3,)), dma((4, n_chunk)), dma((2, n_chunk)), dma((2, n_chunk)),
            dma((3,)), dma((3,)), dma((4,)), dma((4,)), dma((half,)), dma((half,)),
        ] + [dma((half, 3))] * 6 + [dma((half, 7))] * 2,
        compiler_params=pltpu.CompilerParams(
            collective_id=0, has_side_effects=True, vmem_limit_bytes=58 * 1024 * 1024),
    )(doc_bounds, continues, filters, key_proj[0], value_proj[0], query_gate[0], grad_out[0])
    out = pl.pallas_call(
        write_out, out_shape=shapes, in_specs=[pl.BlockSpec(memory_space=pltpu.VMEM)] * 4, out_specs=(pinned,) * 4,
        scratch_shapes=[dma((4, 2))], compiler_params=pltpu.CompilerParams(vmem_limit_bytes=48 * 1024 * 1024),
    )(*mine)
    return out[0][None], out[1][None], out[2][None], out[3]


def solution(mesh):
    n_ctx = mesh.shape["ctx"]
    norm = 1.0 / math.sqrt(mesh.shape["fsdp"] * n_ctx * T)
    wide = P("fsdp", "ctx", "tp")
    return jax.shard_map(
        functools.partial(shards, n_ctx, norm), mesh=mesh,
        in_specs=(wide, wide, wide, wide, P("fsdp", "tp"), P("fsdp", None), P("fsdp", "ctx")),
        out_specs=(wide, wide, wide, P("fsdp", "tp")), check_vma=False)
```
